32 devices in a mesh: arrays: 2 (over y), chan: 4 (over z), win: 4 (over x, core).
Axes of the slice: x: 2, y: 2, z: 4, core: 2. Of those that a mesh axis runs over, the one named last changes fastest.
Arguments:
- traces: float32 [16, 4, 12, 2048], P(('arrays', 'chan'), 'win'), parts along dimension 0
- seg_count: int32 [8], P('arrays'), parts along dimension 0, may hold values from 1 to 12, as said below
Outputs:
- stacked: float32 [8, 2, 2, 2, 1024], P(('arrays', 'chan')), parts along dimension 0
The draws below stay inside these ranges and needn't reach their ends.
There are 2 independent parts, one for each index of `arrays`. The reference program is written for one: setup_inputs(seed, part) draws one part's arguments, and reference() takes and returns one part's arrays. A program takes and returns all parts, laid end to end along the dimension named above; each array names one. Nothing has to cross between parts.
Inputs may be any that keep to these rules, and one draw needn't show every extreme that they name: `seg_count`: every sub-window keeps at least one segment, and some sub-window keeps all 12.
All inputs are finite; a program needn't handle non-finite values.
Results may differ from the reference program's by a relative error of at most 0.0068.
Values may be sent and summed in bfloat16 or wider, within the bound.
No kernel may reach another device: no remote copies, remote signals or barrier semaphores. Data moves between devices by JAX's collectives and lax.ppermute only.
A program may use at most 64 MiB of HBM per device.

```python
import math
import jax
import jax.numpy as jnp
from jax import lax

CH_DEV = 2
SEGS = 12
NFFT = 2048
F = 512
LAGS = 1024
BLOCKS = 4
CHANNELS = 8
WINS = 4


def draw_traces(key, part):
    noise_key = jax.random.fold_in(key, 11)
    scale_key = jax.random.fold_in(key, 12)
    shape = (CHANNELS, WINS, SEGS, NFFT)
    row_scale = jnp.exp(jax.random.uniform(scale_key, (CHANNELS, WINS, SEGS, 1), jnp.float32, 0.0, math.log(10.0)))
    return row_scale * jax.random.normal(noise_key, shape, jnp.float32)


def draw_seg_count(key, part):
    counts = jax.random.randint(jax.random.fold_in(key, 21), (WINS,), 1, SEGS + 1, dtype=jnp.int32)
    full_index = jax.random.randint(jax.random.fold_in(key, 22), (), 0, WINS, dtype=jnp.int32)
    positions = jnp.arange(WINS, dtype=jnp.int32)
    return jnp.where(positions == full_index, SEGS, counts).astype(jnp.int32)


def setup_inputs(seed: int = 0, part: int = 0) -> dict:
    arg_keys = jax.random.split(jax.random.key(seed), 3)
    part_splits = jax.random.split(jax.random.fold_in(arg_keys[2], part), 3)
    return {
        "traces": draw_traces(jax.random.fold_in(jax.random.fold_in(arg_keys[2], part), 71), part),
        "seg_count": draw_seg_count(jax.random.fold_in(jax.random.fold_in(arg_keys[2], part), 71), part),
    }


def forward_table(length, bin_count, lowest_bin):
    sample_index = jnp.arange(length, dtype=jnp.int32)
    bin_index = jnp.arange(bin_count, dtype=jnp.int32) + lowest_bin
    phase_index = sample_index[:, None] * bin_index[None, :] % length
    angles = phase_index.astype(jnp.float32) * (2.0 * math.pi / length)
    return jnp.concatenate([jnp.cos(angles), -jnp.sin(angles)], axis=1)

def inverse_table(length, bin_count, lowest_bin, lag_count):
    bin_index = jnp.arange(bin_count, dtype=jnp.int32) + lowest_bin
    shifts = (jnp.arange(lag_count, dtype=jnp.int32) - lag_count // 2 + length) % length
    phase_index = bin_index[:, None] * shifts[None, :] % length
    angles = phase_index.astype(jnp.float32) * (2.0 * math.pi / length)
    cosine = jnp.cos(angles)
    sine_part = jnp.sin(angles)
    upper_rows = jnp.concatenate([cosine, sine_part], axis=1)
    lower_rows = jnp.concatenate([-sine_part, cosine], axis=1)
    joined = jnp.concatenate([upper_rows, lower_rows], axis=0) / math.sqrt(bin_count)
    return joined.astype(jnp.bfloat16)

def whiten(series, dft_table, bin_count):
    spectra = jnp.dot(series, dft_table, precision=lax.Precision.HIGHEST, preferred_element_type=jnp.float32)
    real_part = spectra[:, :bin_count]
    imag_part = spectra[:, bin_count:]
    spectral_power = real_part * real_part + imag_part * imag_part
    rms_level = jnp.sqrt(lax.optimization_barrier(jnp.mean(spectral_power, axis=1, keepdims=True)) + 1e-06)
    divisor = jnp.maximum(jnp.sqrt(spectral_power), 0.3 * rms_level)
    return (spectra / jnp.concatenate([divisor, divisor], axis=1)).astype(jnp.bfloat16)

def cross_spectra(left_spectra, right_spectra, bin_count):
    left_float = left_spectra.astype(jnp.float32)
    right_float = right_spectra.astype(jnp.float32)
    left_real = left_float[:, None, :, None, :bin_count]
    left_imag = left_float[:, None, :, None, bin_count:]
    right_real = right_float[:, :, None, :, :bin_count]
    right_imag = right_float[:, :, None, :, bin_count:]
    cross_real = left_real * right_real + left_imag * right_imag
    cross_imag = left_imag * right_real - left_real * right_imag
    return jnp.concatenate([cross_real, cross_imag], axis=-1).astype(jnp.bfloat16)

def phase_sums(correlated, seg_weights, lag_count):
    direct = correlated[..., :lag_count]
    quadrature = correlated[..., lag_count:]
    magnitude = jnp.sqrt(direct * direct + quadrature * quadrature)
    divisor = jnp.maximum(magnitude, 0.5)
    weighting = seg_weights[:, None, None]
    linear = lax.optimization_barrier(jnp.sum(weighting * direct, axis=0))
    cos_sum = lax.optimization_barrier(jnp.sum(weighting * (direct / divisor), axis=0))
    sin_sum = lax.optimization_barrier(jnp.sum(weighting * (quadrature / divisor), axis=0))
    return (linear, cos_sum, sin_sum)

def reference(traces, seg_count):
    lowest_bin = NFFT // 16
    forward = forward_table(NFFT, F, lowest_bin)
    backward = inverse_table(NFFT, F, lowest_bin, LAGS).astype(jnp.float32)
    spectra = whiten(traces.reshape(-1, NFFT), forward, F).reshape(BLOCKS, CH_DEV, WINS, SEGS, 2 * F)
    seg_weights = (jnp.arange(SEGS, dtype=jnp.int32)[None, :] < seg_count[:, None]).astype(jnp.float32)
    kept_total = jnp.sum(seg_count).astype(jnp.float32)
    span_blocks = BLOCKS // 2

    def one_block(block_index):
        own_spectra = spectra[block_index]
        visitor_index = ((block_index + 1 + jnp.arange(span_blocks, dtype=jnp.int32)) % BLOCKS).astype(jnp.int32)
        visitors = jnp.take(spectra, visitor_index, axis=0)
        left_spectra = own_spectra.transpose(1, 2, 0, 3).reshape(WINS * SEGS, CH_DEV, 2 * F)
        right_spectra = visitors.transpose(2, 3, 0, 1, 4).reshape(WINS * SEGS, span_blocks, CH_DEV, 2 * F)
        products = cross_spectra(left_spectra, right_spectra, F)
        row_block = products.reshape(-1, 2 * F).astype(jnp.float32)
        correlated = jnp.dot(row_block, backward, precision=lax.Precision.HIGHEST, preferred_element_type=jnp.float32).reshape(WINS * SEGS, -1, 2 * LAGS)
        linear, cos_sum, sin_sum = phase_sums(correlated, seg_weights.reshape(-1), LAGS)
        result = linear * (cos_sum * cos_sum + sin_sum * sin_sum) / (kept_total * kept_total)
        return result.reshape(span_blocks, CH_DEV, CH_DEV, LAGS)
    return lax.map(one_block, jnp.arange(BLOCKS, dtype=jnp.int32))
```

```python
import functools
import math

import jax
import jax.numpy as jnp
import numpy as np
from jax import lax
from jax.experimental import pallas as pl
from jax.experimental.pallas import tpu as pltpu
from jax.sharding import PartitionSpec as P

NFFT = 2048
F = 512
LAGS = 1024
LOWEST = NFFT // 16
LANES = 128

RADIX = 4
PERIOD = NFFT // RADIX
QS = F // RADIX
QUEUE = LOWEST // RADIX + np.arange(QS)

VMEM = pl.BlockSpec(memory_space=pltpu.VMEM)


def split_three(table):
    parts = []
    rest = np.asarray(table, np.float64)
    for _ in range(3):
        part = rest.astype(np.float32).astype(jnp.bfloat16)
        parts.append(part)
        rest = rest - part.astype(np.float64)
    return parts


def forward_tables():
    t0 = np.arange(PERIOD)
    angle = (t0[:, None] * QUEUE[None, :] % PERIOD) * (2 * math.pi / PERIOD)
    cosine, sine = np.cos(angle), np.sin(angle)
    return split_three(np.block([[cosine, -sine], [sine, cosine]]))


def backward_table():
    m = np.arange(PERIOD)
    angle = (QUEUE[:, None] * m[None, :] % PERIOD) * (2 * math.pi / PERIOD)
    cosine, sine = np.cos(angle), np.sin(angle)
    table = np.block([[cosine, sine], [-sine, cosine]]) / math.sqrt(F)
    return table.astype(np.float32).astype(jnp.bfloat16)


def twiddles():
    n = np.arange(PERIOD)
    rows = []
    for r in range(1, RADIX):
        angle = (r * n) * (2 * math.pi / NFFT)
        rows += [np.cos(angle), np.sin(angle)]
    rows += [np.zeros(PERIOD)] * 2
    return np.stack(rows).astype(np.float32)


def whiten_kernel(rows, x_ref, high_ref, mid_ref, low_ref, twiddle_ref, out_ref):
    chunks = PERIOD // LANES
    stride = NFFT // LANES
    real = [[] for _ in range(RADIX)]
    imag = [[] for _ in range(RADIX)]
    for c in range(chunks):
        x0, x1, x2, x3 = (
            x_ref[pl.ds(t1 * chunks + c, rows, stride=stride), :] for t1 in range(RADIX)
        )
        cos1, sin1, cos2, sin2, cos3, sin3 = (
            twiddle_ref[i : i + 1, c * LANES : (c + 1) * LANES] for i in range(6)
        )
        even, odd = x0 + x2, x1 + x3
        a, b = x0 - x2, x1 - x3
        both = even - odd
        real[0].append(even + odd)
        imag[0].append(jnp.zeros_like(even))
        real[1].append(a * cos1 - b * sin1)
        imag[1].append(-(a * sin1 + b * cos1))
        real[2].append(both * cos2)
        imag[2].append(-(both * sin2))
        real[3].append(a * cos3 + b * sin3)
        imag[3].append(b * cos3 - a * sin3)
    series = jnp.concatenate(
        [jnp.concatenate(real[r] + imag[r], axis=1) for r in range(RADIX)], axis=0
    )
    high = series.astype(jnp.bfloat16)
    rest = series - high.astype(jnp.float32)
    mid = rest.astype(jnp.bfloat16)
    low = (rest - mid.astype(jnp.float32)).astype(jnp.bfloat16)
    dot = functools.partial(jnp.dot, preferred_element_type=jnp.float32)
    n = RADIX * rows
    by_high = dot(jnp.concatenate([high, mid, low], axis=0), high_ref[...])
    by_mid = dot(jnp.concatenate([high, mid], axis=0), mid_ref[...])
    by_low = dot(high, low_ref[...])
    small = by_high[2 * n :] + by_mid[n:] + by_low
    spectra = by_high[:n] + ((by_high[n : 2 * n] + by_mid[:n]) + small)
    power = []
    for r in range(RADIX):
        block = spectra[r * rows : (r + 1) * rows]
        power.append(block[:, :QS] * block[:, :QS] + block[:, QS:] * block[:, QS:])
    total = (power[0] + power[1]) + (power[2] + power[3])
    mean = jnp.sum(total, axis=1, keepdims=True) * (1.0 / F)
    floor = 0.09 * (mean + 1e-06)
    for r in range(RADIX):
        block = spectra[r * rows : (r + 1) * rows]
        scale = lax.rsqrt(jnp.maximum(power[r], floor))
        at = 2 * r * QS
        out_ref[:, at : at + QS] = (block[:, :QS] * scale).astype(jnp.bfloat16)
        out_ref[:, at + QS : at + 2 * QS] = (block[:, QS:] * scale).astype(jnp.bfloat16)


def stack_kernel(
    channels,
    segments,
    own_ref,
    first_ref,
    second_ref,
    count_ref,
    table_ref,
    twiddle_ref,
    out_ref,
    own,
    visitor,
    inner,
):
    rows = channels * segments
    pairs = 2 * channels * channels
    own[...] = own_ref[...].astype(jnp.float32)
    visitor[0:rows] = first_ref[...].astype(jnp.float32)
    visitor[rows : 2 * rows] = second_ref[...].astype(jnp.float32)

    place = lax.broadcasted_iota(jnp.int32, (pairs, LANES), 0)
    a_of = place // channels % channels
    sb_of = place // (channels * channels) * channels + place % channels

    def spread(ref, which, choice, count, segment, at):
        value = None
        for i in range(count):
            row = ref[i * segments + segment, pl.ds(at, LANES)]
            row = jnp.broadcast_to(row.reshape(1, LANES), (pairs, LANES))
            value = row if value is None else jnp.where(choice == i, row, value)
        return value

    for r in range(RADIX):
        cross_real, cross_imag = [], []
        at = 2 * r * QS
        for k in range(segments):
            own_re = spread(own, 0, a_of, channels, k, at)
            own_im = spread(own, 0, a_of, channels, k, at + QS)
            vis_re = spread(visitor, 0, sb_of, 2 * channels, k, at)
            vis_im = spread(visitor, 0, sb_of, 2 * channels, k, at + QS)
            cross_real.append(own_re * vis_re + own_im * vis_im)
            cross_imag.append(own_im * vis_re - own_re * vis_im)
        cross = jnp.concatenate(
            [jnp.concatenate(cross_real, axis=0), jnp.concatenate(cross_imag, axis=0)],
            axis=1,
        ).astype(jnp.bfloat16)
        inner[r] = jnp.dot(cross, table_ref[...], preferred_element_type=jnp.float32)

    window = lax.axis_index("win")
    counts = count_ref[...]
    lane = lax.broadcasted_iota(jnp.int32, counts.shape, 1)
    kept_count = jnp.sum(jnp.where(lane == window, counts, 0), axis=1, keepdims=True)
    kept = [
        jnp.broadcast_to((kept_count > k).astype(jnp.float32), (pairs, LANES))
        for k in range(segments)
    ]

    for c in range(PERIOD // LANES):
        low, high = c * LANES, (c + 1) * LANES
        cos1, sin1, cos2, sin2, cos3, sin3 = (
            jnp.broadcast_to(twiddle_ref[i : i + 1, low:high], (pairs, LANES))
            for i in range(6)
        )
        sums = [[None] * 3, [None] * 3]
        for k in range(segments):
            at = slice(k * pairs, (k + 1) * pairs)
            re = [inner[r, at, low:high] for r in range(RADIX)]
            im = [inner[r, at, PERIOD + low : PERIOD + high] for r in range(RADIX)]
            re1, im1 = re[1] * cos1 - im[1] * sin1, re[1] * sin1 + im[1] * cos1
            re2, im2 = re[2] * cos2 - im[2] * sin2, re[2] * sin2 + im[2] * cos2
            re3, im3 = re[3] * cos3 - im[3] * sin3, re[3] * sin3 + im[3] * cos3
            later = (re[0] + re2) + (re1 + re3), (im[0] + im2) + (im1 + im3)
            earlier = (re[0] - re2) + (im1 - im3), (im[0] - im2) - (re1 - re3)
            for half, (direct, quadrature) in enumerate((earlier, later)):
                power = direct * direct + quadrature * quadrature
                scale = lax.rsqrt(jnp.maximum(power, 0.25)) * kept[k]
                terms = (direct * kept[k], direct * scale, quadrature * scale)
                for i, term in enumerate(terms):
                    old = sums[half][i]
                    sums[half][i] = term if old is None else old + term
        for half in range(2):
            for i in range(3):
                out_ref[
                    i * pairs : (i + 1) * pairs,
                    half * PERIOD + low : half * PERIOD + high,
                ] = sums[half][i]


def add_kernel(left_ref, right_ref, out_ref):
    out_ref[...] = left_ref[...] + right_ref[...]


def final_kernel(shape, left_ref, right_ref, count_ref, out_ref):
    total = jnp.sum(count_ref[...], axis=1, keepdims=True).astype(jnp.float32)
    square = total * total
    groups, offsets = shape
    _, _, channels, _, _ = out_ref.shape
    pairs = offsets * channels * channels
    for g in range(groups):
        at = 3 * pairs * g
        linear, cos_sum, sin_sum = (
            left_ref[at + i * pairs : at + (i + 1) * pairs]
            + right_ref[at + i * pairs : at + (i + 1) * pairs]
            for i in range(3)
        )
        result = linear * (cos_sum * cos_sum + sin_sum * sin_sum) / square
        for s in range(offsets):
            for a in range(channels):
                row = (s * channels + a) * channels
                out_ref[0, g * offsets + s, a] = result[row : row + channels]


def call(kernel, out, *args, scratch=(), limit=8 << 20):
    return pl.pallas_call(
        kernel,
        out_shape=out,
        in_specs=[VMEM] * len(args),
        out_specs=VMEM,
        scratch_shapes=list(scratch),
        compiler_params=pltpu.CompilerParams(vmem_limit_bytes=limit),
    )(*args)


def passed_along(array, axis, by):
    length = lax.axis_size(axis)
    return lax.ppermute(array, axis, [(i, (i + by) % length) for i in range(length)])


def shards(traces, seg_count):
    channels, _, segments, _ = traces.shape
    rows = channels * segments
    span_blocks = lax.axis_size("chan") // 2
    windows = lax.axis_size("win")
    twiddle = jnp.asarray(twiddles())

    own = call(
        functools.partial(whiten_kernel, rows),
        jax.ShapeDtypeStruct((rows, 2 * F), jnp.bfloat16),
        traces.reshape(-1, LANES),
        *(jnp.asarray(part) for part in forward_tables()),
        twiddle,
    )

    visitors = [passed_along(own, "chan", -1 - s) for s in range(min(span_blocks, 2))]
    if span_blocks > 2:
        collected = jnp.stack(visitors)
        while collected.shape[0] < span_blocks:
            held = collected.shape[0]
            more = min(held, span_blocks - held)
            arrived = passed_along(collected[:more], "chan", -held)
            collected = jnp.concatenate([collected, arrived], axis=0)
        visitors = [collected[s] for s in range(span_blocks)]

    counts = seg_count.reshape(1, -1)
    backward = jnp.asarray(backward_table())
    pairs = 2 * channels * channels
    stacks = [
        call(
            functools.partial(stack_kernel, channels, segments),
            jax.ShapeDtypeStruct((3 * pairs, LAGS), jnp.float32),
            own,
            visitors[s],
            visitors[s + 1],
            counts,
            backward,
            twiddle,
            scratch=(
                pltpu.VMEM((rows, 2 * F), jnp.float32),
                pltpu.VMEM((2 * rows, 2 * F), jnp.float32),
                pltpu.VMEM((RADIX, segments * pairs, LAGS), jnp.float32),
            ),
        )
        for s in range(0, span_blocks, 2)
    ]
    stack = stacks[0] if len(stacks) == 1 else jnp.concatenate(stacks, axis=0)

    step = 1
    while True:
        arrived = lax.ppermute(stack, "win", [(i, i ^ step) for i in range(windows)])
        step *= 2
        if step == windows:
            break
        stack = call(
            add_kernel, jax.ShapeDtypeStruct(stack.shape, jnp.float32), stack, arrived
        )
    return call(
        functools.partial(final_kernel, (span_blocks // 2, 2)),
        jax.ShapeDtypeStruct((1, span_blocks, channels, channels, LAGS), jnp.float32),
        stack,
        arrived,
        counts,
    )


def solution(mesh):
    placed = (P(("arrays", "chan"), "win", None, None), P("arrays"))
    return jax.shard_map(
        shards,
        mesh=mesh,
        in_specs=placed,
        out_specs=P(("arrays", "chan"), None, None, None, None),
        check_vma=False,
    )
```

```python
import functools
import math

import jax
import jax.numpy as jnp
import numpy as np
from jax import lax
from jax.experimental import pallas as pl
from jax.experimental.pallas import tpu as pltpu
from jax.sharding import PartitionSpec as P

NFFT = 2048
F = 512
LAGS = 1024
LOWEST = NFFT // 16
LANES = 128

RADIX = 4
PERIOD = NFFT // RADIX
QS = F // RADIX
QUEUE = LOWEST // RADIX + np.arange(QS)

VMEM = pl.BlockSpec(memory_space=pltpu.VMEM)
HBM = pl.BlockSpec(memory_space=pltpu.HBM)


def split_three(table):
    parts = []
    rest = np.asarray(table, np.float64)
    for _ in range(3):
        part = rest.astype(np.float32).astype(jnp.bfloat16)
        parts.append(part)
        rest = rest - part.astype(np.float64)
    return parts


def forward_tables():
    t0 = np.arange(PERIOD)
    angle = (t0[:, None] * QUEUE[None, :] % PERIOD) * (2 * math.pi / PERIOD)
    cosine, sine = np.cos(angle), np.sin(angle)
    return split_three(np.block([[cosine, -sine], [sine, cosine]]))


def backward_table():
    m = np.arange(PERIOD)
    angle = (QUEUE[:, None] * m[None, :] % PERIOD) * (2 * math.pi / PERIOD)
    cosine, sine = np.cos(angle), np.sin(angle)
    table = np.block([[cosine, sine], [-sine, cosine]]) / math.sqrt(F)
    return table.astype(np.float32).astype(jnp.bfloat16)


def twiddles():
    n = np.arange(PERIOD)
    rows = []
    for r in range(1, RADIX):
        angle = (r * n) * (2 * math.pi / NFFT)
        rows += [np.cos(angle), np.sin(angle)]
    rows += [np.zeros(PERIOD)] * 2
    return np.stack(rows).astype(np.float32)


def whiten_kernel(
    rows, x_hbm, tables_hbm, twiddle_hbm, out_ref, x_ref, tables, twiddle_ref, sems
):
    copies = [
        pltpu.make_async_copy(x_hbm, x_ref, sems.at[0]),
        pltpu.make_async_copy(twiddle_hbm, twiddle_ref, sems.at[1]),
    ]
    copies += [
        pltpu.make_async_copy(tables_hbm.at[i], tables.at[i], sems.at[2 + i])
        for i in range(3)
    ]
    for copy in copies:
        copy.start()
    copies[0].wait()
    copies[1].wait()

    chunks = PERIOD // LANES
    stride = NFFT // LANES
    real = [[] for _ in range(RADIX)]
    imag = [[] for _ in range(RADIX)]
    for c in range(chunks):
        x0, x1, x2, x3 = (
            x_ref[pl.ds(t1 * chunks + c, rows, stride=stride), :] for t1 in range(RADIX)
        )
        cos1, sin1, cos2, sin2, cos3, sin3 = (
            twiddle_ref[i : i + 1, c * LANES : (c + 1) * LANES] for i in range(6)
        )
        even, odd = x0 + x2, x1 + x3
        a, b = x0 - x2, x1 - x3
        both = even - odd
        real[0].append(even + odd)
        imag[0].append(jnp.zeros_like(even))
        real[1].append(a * cos1 - b * sin1)
        imag[1].append(-(a * sin1 + b * cos1))
        real[2].append(both * cos2)
        imag[2].append(-(both * sin2))
        real[3].append(a * cos3 + b * sin3)
        imag[3].append(b * cos3 - a * sin3)
    series = jnp.concatenate(
        [jnp.concatenate(real[r] + imag[r], axis=1) for r in range(RADIX)], axis=0
    )
    high = series.astype(jnp.bfloat16)
    rest = series - high.astype(jnp.float32)
    mid = rest.astype(jnp.bfloat16)
    low = (rest - mid.astype(jnp.float32)).astype(jnp.bfloat16)
    dot = functools.partial(jnp.dot, preferred_element_type=jnp.float32)
    n = RADIX * rows
    copies[2].wait()
    by_high = dot(jnp.concatenate([high, mid, low], axis=0), tables[0])
    copies[3].wait()
    by_mid = dot(jnp.concatenate([high, mid], axis=0), tables[1])
    copies[4].wait()
    by_low = dot(high, tables[2])
    small = by_high[2 * n :] + by_mid[n:] + by_low
    spectra = by_high[:n] + ((by_high[n : 2 * n] + by_mid[:n]) + small)
    power = []
    for r in range(RADIX):
        block = spectra[r * rows : (r + 1) * rows]
        power.append(block[:, :QS] * block[:, :QS] + block[:, QS:] * block[:, QS:])
    total = (power[0] + power[1]) + (power[2] + power[3])
    mean = jnp.sum(total, axis=1, keepdims=True) * (1.0 / F)
    floor = 0.09 * (mean + 1e-06)
    for r in range(RADIX):
        block = spectra[r * rows : (r + 1) * rows]
        scale = lax.rsqrt(jnp.maximum(power[r], floor))
        at = 2 * r * QS
        out_ref[:, at : at + QS] = (block[:, :QS] * scale).astype(jnp.bfloat16)
        out_ref[:, at + QS : at + 2 * QS] = (block[:, QS:] * scale).astype(jnp.bfloat16)


def stack_kernel(
    channels,
    segments,
    own_ref,
    own_mate_ref,
    visitor_ref,
    visitor_mate_ref,
    count_ref,
    table_ref,
    twiddle_ref,
    out_ref,
    own,
    visitor,
    inner,
):
    rows = channels * segments
    pairs = channels * channels
    group = 2 * pairs
    own[0:rows] = own_ref[...].astype(jnp.float32)
    own[rows : 2 * rows] = own_mate_ref[...].astype(jnp.float32)
    visitor[0:rows] = visitor_ref[...].astype(jnp.float32)
    visitor[rows : 2 * rows] = visitor_mate_ref[...].astype(jnp.float32)

    place = lax.broadcasted_iota(jnp.int32, (group, LANES), 0)
    own_of = place // channels
    visitor_of = place // pairs * channels + place % channels
    is_own = place < pairs

    def spread(ref, choice, segment, at):
        value = None
        for i in range(2 * channels):
            row = ref[pl.ds(i * segments + segment, 1), pl.ds(at, LANES)]
            row = jnp.broadcast_to(row, (group, LANES))
            value = row if value is None else jnp.where(choice == i, row, value)
        return value

    for r in range(RADIX):
        cross_real, cross_imag = [], []
        at = 2 * r * QS
        for k in range(segments):
            own_re = spread(own, own_of, k, at)
            own_im = spread(own, own_of, k, at + QS)
            vis_re = spread(visitor, visitor_of, k, at)
            vis_im = spread(visitor, visitor_of, k, at + QS)
            cross_real.append(own_re * vis_re + own_im * vis_im)
            cross_imag.append(own_im * vis_re - own_re * vis_im)
        cross = jnp.concatenate(
            [jnp.concatenate(cross_real, axis=0), jnp.concatenate(cross_imag, axis=0)],
            axis=1,
        ).astype(jnp.bfloat16)
        inner[r] = jnp.dot(cross, table_ref[...], preferred_element_type=jnp.float32)

    window = lax.axis_index("win")
    mate = window + 1 - 2 * (window % 2)
    counts = count_ref[...]
    lane = lax.broadcasted_iota(jnp.int32, counts.shape, 1)
    kept_own, kept_mate = (
        jnp.sum(jnp.where(lane == w, counts, 0), axis=1, keepdims=True)
        for w in (window, mate)
    )
    kept_count = jnp.where(is_own, kept_own, kept_mate)
    kept = [(kept_count > k).astype(jnp.float32) for k in range(segments)]

    for c in range(PERIOD // LANES):
        low, high = c * LANES, (c + 1) * LANES
        cos1, sin1, cos2, sin2, cos3, sin3 = (
            jnp.broadcast_to(twiddle_ref[i : i + 1, low:high], (group, LANES))
            for i in range(6)
        )
        sums = [[None] * 3, [None] * 3]
        for k in range(segments):
            at = slice(k * group, (k + 1) * group)
            re = [inner[r, at, low:high] for r in range(RADIX)]
            im = [inner[r, at, PERIOD + low : PERIOD + high] for r in range(RADIX)]
            re1, im1 = re[1] * cos1 - im[1] * sin1, re[1] * sin1 + im[1] * cos1
            re2, im2 = re[2] * cos2 - im[2] * sin2, re[2] * sin2 + im[2] * cos2
            re3, im3 = re[3] * cos3 - im[3] * sin3, re[3] * sin3 + im[3] * cos3
            later = (re[0] + re2) + (re1 + re3), (im[0] + im2) + (im1 + im3)
            earlier = (re[0] - re2) + (im1 - im3), (im[0] - im2) - (re1 - re3)
            for half, (direct, quadrature) in enumerate((earlier, later)):
                power = direct * direct + quadrature * quadrature
                scale = lax.rsqrt(jnp.maximum(power, 0.25)) * kept[k]
                terms = (direct * kept[k], direct * scale, quadrature * scale)
                for i, term in enumerate(terms):
                    old = sums[half][i]
                    sums[half][i] = term if old is None else old + term
        for i in range(3):
            first, second = (
                sums[half][i] + pltpu.roll(sums[half][i], pairs, axis=0)
                for half in range(2)
            )
            out_ref[i * group : (i + 1) * group, low:high] = jnp.where(
                is_own, first, second
            )


def add_kernel(left_ref, right_ref, out_ref):
    out_ref[...] = left_ref[...] + right_ref[...]


def result_kernel(left_ref, right_ref, count_ref, out_ref):
    total = jnp.sum(count_ref[...], axis=1, keepdims=True).astype(jnp.float32)
    square = total * total
    group = out_ref.shape[1]
    for offset in range(out_ref.shape[0]):
        linear, cos_sum, sin_sum = (
            left_ref[offset, i * group : (i + 1) * group]
            + right_ref[offset, i * group : (i + 1) * group]
            for i in range(3)
        )
        out_ref[offset] = linear * (cos_sum * cos_sum + sin_sum * sin_sum) / square


def join_kernel(own_ref, mate_ref, out_ref):
    core = lax.axis_index("win") % 2
    channels = out_ref.shape[2]
    half_lags = own_ref.shape[2]
    for ref, parity in ((own_ref, core), (mate_ref, 1 - core)):
        for offset in range(own_ref.shape[0]):
            for half in range(2):
                for a in range(channels):
                    row = (half * channels + a) * channels
                    lags = slice(half * half_lags, (half + 1) * half_lags)
                    out_ref[0, 2 * offset + parity, a, :, lags] = ref[
                        offset, row : row + channels
                    ]


def call(kernel, out, *args, specs=None, scratch=(), limit=8 << 20):
    return pl.pallas_call(
        kernel,
        out_shape=out,
        in_specs=[VMEM] * len(args) if specs is None else specs,
        out_specs=VMEM,
        scratch_shapes=list(scratch),
        compiler_params=pltpu.CompilerParams(vmem_limit_bytes=limit),
    )(*args)


def shards(traces, seg_count):
    channels, _, segments, _ = traces.shape
    rows = channels * segments
    blocks = lax.axis_size("chan")
    windows = lax.axis_size("win")
    offsets = blocks // 4
    pairs = channels * channels
    group = 2 * pairs
    twiddle = jnp.asarray(twiddles())
    tables = jnp.asarray(np.stack(forward_tables()))
    series = traces.reshape(-1, LANES)

    own = call(
        functools.partial(whiten_kernel, rows),
        jax.ShapeDtypeStruct((rows, 2 * F), jnp.bfloat16),
        *(pltpu.with_memory_space_constraint(x, pltpu.HBM) for x in (series, tables, twiddle)),
        specs=[HBM] * 3,
        scratch=(
            pltpu.VMEM(series.shape, jnp.float32),
            pltpu.VMEM(tables.shape, jnp.bfloat16),
            pltpu.VMEM(twiddle.shape, jnp.float32),
            pltpu.SemaphoreType.DMA((5,)),
        ),
    )

    def to_mate(array):
        return lax.ppermute(array, "win", [(w, w ^ 1) for w in range(windows)])

    def from_block(array, offset, flip):
        moves = []
        for z in range(blocks):
            for w in range(windows):
                source = (z + offset + w % 2) % blocks * windows + (w ^ flip)
                moves.append((source, z * windows + w))
        return lax.ppermute(array, ("chan", "win"), moves)

    counts = seg_count.reshape(1, -1)
    backward = jnp.asarray(backward_table())
    own_mate = to_mate(own)
    stacks = []
    for j in range(offsets):
        visitor = from_block(own, 1 + 2 * j, 0)
        visitor_mate = from_block(own, 1 + 2 * j, 1)
        stacks.append(
            call(
                functools.partial(stack_kernel, channels, segments),
                jax.ShapeDtypeStruct((3 * group, PERIOD), jnp.float32),
                own,
                own_mate,
                visitor,
                visitor_mate,
                counts,
                backward,
                twiddle,
                scratch=(
                    pltpu.VMEM((2 * rows, 2 * F), jnp.float32),
                    pltpu.VMEM((2 * rows, 2 * F), jnp.float32),
                    pltpu.VMEM((RADIX, segments * group, 2 * PERIOD), jnp.float32),
                ),
            )
        )
    stack = jnp.stack(stacks)

    step = 2
    while True:
        arrived = lax.ppermute(stack, "win", [(w, w ^ step) for w in range(windows)])
        step *= 2
        if step == windows:
            break
        stack = call(
            add_kernel, jax.ShapeDtypeStruct(stack.shape, jnp.float32), stack, arrived
        )
    result = call(
        result_kernel,
        jax.ShapeDtypeStruct((offsets, group, PERIOD), jnp.float32),
        stack,
        arrived,
        counts,
    )
    return call(
        join_kernel,
        jax.ShapeDtypeStruct((1, 2 * offsets, channels, channels, LAGS), jnp.float32),
        result,
        to_mate(result),
    )


def solution(mesh):
    placed = (P(("arrays", "chan"), "win", None, None), P("arrays"))
    return jax.shard_map(
        shards,
        mesh=mesh,
        in_specs=placed,
        out_specs=P(("arrays", "chan"), None, None, None, None),
        check_vma=False,
    )
```

```python
import functools
import math

import jax
import jax.numpy as jnp
import numpy as np
from jax import lax
from jax.experimental import pallas as pl
from jax.experimental.pallas import tpu as pltpu
from jax.sharding import PartitionSpec as P

NFFT = 2048
F = 512
LAGS = 1024
LOWEST = NFFT // 16
LANES = 128

RADIX = 4
PERIOD = NFFT // RADIX
QS = F // RADIX
SPLIT = 8
SPAN = NFFT // SPLIT
NARROW = F // SPLIT
FORWARD_Q = LOWEST // SPLIT + np.arange(NARROW)
BACKWARD_Q = np.concatenate([2 * FORWARD_Q, 2 * FORWARD_Q + 1])

VMEM = pl.BlockSpec(memory_space=pltpu.VMEM)
HBM = pl.BlockSpec(memory_space=pltpu.HBM)


def split_three(table):
    parts = []
    rest = np.asarray(table, np.float64)
    for _ in range(3):
        part = rest.astype(np.float32).astype(jnp.bfloat16)
        parts.append(part)
        rest = rest - part.astype(np.float64)
    return parts


def forward_tables():
    t0 = np.arange(SPAN)
    angle = (t0[:, None] * FORWARD_Q[None, :] % SPAN) * (2 * math.pi / SPAN)
    cosine, sine = np.cos(angle), np.sin(angle)
    return split_three(np.block([[cosine, -sine], [sine, cosine]]))


def backward_table():
    m = np.arange(PERIOD)
    angle = (BACKWARD_Q[:, None] * m[None, :] % PERIOD) * (2 * math.pi / PERIOD)
    table = np.block([np.cos(angle), np.sin(angle)]) / math.sqrt(F)
    return table.astype(np.float32).astype(jnp.bfloat16)


def twiddles(count, length):
    n = np.arange(length)
    rows = []
    for r in range(1, count):
        angle = (r * n) * (2 * math.pi / NFFT)
        rows += [np.cos(angle), np.sin(angle)]
    rows += [np.zeros(length)] * 2
    return np.stack(rows).astype(np.float32)


def eight_points(x):
    half = math.sqrt(0.5)
    s04, d04, s26, d26 = x[0] + x[4], x[0] - x[4], x[2] + x[6], x[2] - x[6]
    s15, d15, s37, d37 = x[1] + x[5], x[1] - x[5], x[3] + x[7], x[3] - x[7]
    even, odd = s04 + s26, s15 + s37
    plus, minus = (d15 + d37) * half, (d15 - d37) * half
    two = s04 - s26, s37 - s15
    one = d04 + minus, -(d26 + plus)
    three = d04 - minus, d26 - plus
    return [
        (even + odd, None),
        one,
        two,
        three,
        (even - odd, None),
        (three[0], -three[1]),
        (two[0], -two[1]),
        (one[0], -one[1]),
    ]


def whiten_kernel(
    rows, x_hbm, tables_hbm, twiddle_hbm, out_ref, x_ref, tables, twiddle_ref, sems
):
    copies = [
        pltpu.make_async_copy(x_hbm, x_ref, sems.at[0]),
        pltpu.make_async_copy(twiddle_hbm, twiddle_ref, sems.at[1]),
    ]
    copies += [
        pltpu.make_async_copy(tables_hbm.at[i], tables.at[i], sems.at[2 + i])
        for i in range(3)
    ]
    for copy in copies:
        copy.start()
    for copy in copies:
        copy.wait()

    chunks = SPAN // LANES
    real = [[] for _ in range(SPLIT)]
    imag = [[] for _ in range(SPLIT)]
    for c in range(chunks):
        x = [
            x_ref[pl.ds(t1 * chunks + c, rows, stride=SPLIT * chunks), :]
            for t1 in range(SPLIT)
        ]
        for r, (re, im) in enumerate(eight_points(x)):
            if r > 0:
                cosine, sine = (
                    twiddle_ref[2 * r - 2 + i, c * LANES : (c + 1) * LANES].reshape(1, LANES)
                    for i in range(2)
                )
                if im is None:
                    re, im = re * cosine, -(re * sine)
                else:
                    re, im = re * cosine + im * sine, im * cosine - re * sine
            real[r].append(re)
            imag[r].append(jnp.zeros_like(re) if im is None else im)
    series = jnp.concatenate(
        [jnp.concatenate(real[r] + imag[r], axis=1) for r in range(SPLIT)], axis=0
    )
    high = series.astype(jnp.bfloat16)
    rest = series - high.astype(jnp.float32)
    mid = rest.astype(jnp.bfloat16)
    low = (rest - mid.astype(jnp.float32)).astype(jnp.bfloat16)
    dot = functools.partial(jnp.dot, preferred_element_type=jnp.float32)
    n = SPLIT * rows
    by_high = dot(jnp.concatenate([high, mid, low], axis=0), tables[0])
    by_mid = dot(jnp.concatenate([high, mid], axis=0), tables[1])
    by_low = dot(high, tables[2])
    small = by_high[2 * n :] + by_mid[n:] + by_low
    spectra = by_high[:n] + ((by_high[n : 2 * n] + by_mid[:n]) + small)
    blocks = [spectra[r * rows : (r + 1) * rows] for r in range(SPLIT)]
    power = []
    for block in blocks:
        square = block * block
        power.append(square + pltpu.roll(square, NARROW, axis=1))
    total = ((power[0] + power[1]) + (power[2] + power[3])) + (
        (power[4] + power[5]) + (power[6] + power[7])
    )
    mean = jnp.sum(total, axis=1, keepdims=True) * (0.5 / F)
    floor = 0.09 * (mean + 1e-06)
    left = lax.broadcasted_iota(jnp.int32, (rows, LANES), 1) < NARROW
    white = [b * lax.rsqrt(jnp.maximum(p, floor)) for b, p in zip(blocks, power)]
    for r in range(RADIX):
        first, second = white[r], white[r + RADIX]
        at = 2 * r * QS
        re = jnp.where(left, first, pltpu.roll(second, NARROW, axis=1))
        im = jnp.where(left, pltpu.roll(first, NARROW, axis=1), second)
        out_ref[:, at : at + QS] = re.astype(jnp.bfloat16)
        out_ref[:, at + QS : at + 2 * QS] = im.astype(jnp.bfloat16)


def stack_kernel(
    channels,
    segments,
    own_ref,
    own_mate_ref,
    visitor_ref,
    visitor_mate_ref,
    count_ref,
    table_ref,
    twiddle_ref,
    out_ref,
    own,
    visitor,
    table,
    inner,
):
    rows = channels * segments
    pairs = channels * channels
    group = 2 * pairs
    own[0:rows] = own_ref[...].astype(jnp.float32)
    own[rows : 2 * rows] = own_mate_ref[...].astype(jnp.float32)
    visitor[0:rows] = visitor_ref[...].astype(jnp.float32)
    visitor[rows : 2 * rows] = visitor_mate_ref[...].astype(jnp.float32)

    table[0:QS] = table_ref[...]
    table[QS : 2 * QS, 0:PERIOD] = -table_ref[:, PERIOD:]
    table[QS : 2 * QS, PERIOD:] = table_ref[:, 0:PERIOD]

    place = lax.broadcasted_iota(jnp.int32, (group, LANES), 0)
    own_of = place // channels
    visitor_of = place // pairs * channels + place % channels
    is_own = place < pairs

    def spread(ref, choice, segment, at):
        value = None
        for i in range(2 * channels):
            row = ref[pl.ds(i * segments + segment, 1), pl.ds(at, LANES)]
            row = jnp.broadcast_to(row, (group, LANES))
            value = row if value is None else jnp.where(choice == i, row, value)
        return value

    for r in range(RADIX):
        cross_real, cross_imag = [], []
        at = 2 * r * QS
        for k in range(segments):
            own_re = spread(own, own_of, k, at)
            own_im = spread(own, own_of, k, at + QS)
            vis_re = spread(visitor, visitor_of, k, at)
            vis_im = spread(visitor, visitor_of, k, at + QS)
            cross_real.append(own_re * vis_re + own_im * vis_im)
            cross_imag.append(own_im * vis_re - own_re * vis_im)
        cross = jnp.concatenate(
            [jnp.concatenate(cross_real, axis=0), jnp.concatenate(cross_imag, axis=0)],
            axis=1,
        ).astype(jnp.bfloat16)
        inner[r] = jnp.dot(cross, table[...], preferred_element_type=jnp.float32)

    window = lax.axis_index("win")
    mate = window + 1 - 2 * (window % 2)
    counts = count_ref[...]
    lane = lax.broadcasted_iota(jnp.int32, counts.shape, 1)
    kept_own, kept_mate = (
        jnp.sum(jnp.where(lane == w, counts, 0), axis=1, keepdims=True)
        for w in (window, mate)
    )
    kept_count = jnp.where(is_own, kept_own, kept_mate)
    kept = [(kept_count > k).astype(jnp.float32) for k in range(segments)]

    for c in range(PERIOD // LANES):
        low, high = c * LANES, (c + 1) * LANES
        cos1, sin1, cos2, sin2, cos3, sin3 = (
            jnp.broadcast_to(twiddle_ref[i : i + 1, low:high], (group, LANES))
            for i in range(6)
        )
        sums = [[None] * 3, [None] * 3]
        for k in range(segments):
            at = slice(k * group, (k + 1) * group)
            re = [inner[r, at, low:high] for r in range(RADIX)]
            im = [inner[r, at, PERIOD + low : PERIOD + high] for r in range(RADIX)]
            re1, im1 = re[1] * cos1 - im[1] * sin1, re[1] * sin1 + im[1] * cos1
            re2, im2 = re[2] * cos2 - im[2] * sin2, re[2] * sin2 + im[2] * cos2
            re3, im3 = re[3] * cos3 - im[3] * sin3, re[3] * sin3 + im[3] * cos3
            later = (re[0] + re2) + (re1 + re3), (im[0] + im2) + (im1 + im3)
            earlier = (re[0] - re2) + (im1 - im3), (im[0] - im2) - (re1 - re3)
            for half, (direct, quadrature) in enumerate((earlier, later)):
                power = direct * direct + quadrature * quadrature
                scale = lax.rsqrt(jnp.maximum(power, 0.25)) * kept[k]
                terms = (direct * kept[k], direct * scale, quadrature * scale)
                for i, term in enumerate(terms):
                    old = sums[half][i]
                    sums[half][i] = term if old is None else old + term
        for i in range(3):
            first, second = (
                sums[half][i] + pltpu.roll(sums[half][i], pairs, axis=0)
                for half in range(2)
            )
            out_ref[i * group : (i + 1) * group, low:high] = jnp.where(
                is_own, first, second
            )


def add_kernel(left_ref, right_ref, out_ref):
    out_ref[...] = left_ref[...] + right_ref[...]


def result_kernel(left_ref, right_ref, count_ref, out_ref):
    total = jnp.sum(count_ref[...], axis=1, keepdims=True).astype(jnp.float32)
    square = total * total
    group = out_ref.shape[1]
    for offset in range(out_ref.shape[0]):
        linear, cos_sum, sin_sum = (
            left_ref[offset, i * group : (i + 1) * group]
            + right_ref[offset, i * group : (i + 1) * group]
            for i in range(3)
        )
        out_ref[offset] = linear * (cos_sum * cos_sum + sin_sum * sin_sum) / square


def join_kernel(own_ref, mate_ref, out_ref):
    core = lax.axis_index("win") % 2
    channels = out_ref.shape[2]
    half_lags = own_ref.shape[2]
    for ref, parity in ((own_ref, core), (mate_ref, 1 - core)):
        for offset in range(own_ref.shape[0]):
            for half in range(2):
                for a in range(channels):
                    row = (half * channels + a) * channels
                    lags = slice(half * half_lags, (half + 1) * half_lags)
                    out_ref[0, 2 * offset + parity, a, :, lags] = ref[
                        offset, row : row + channels
                    ]


def call(kernel, out, *args, specs=None, scratch=(), limit=8 << 20):
    return pl.pallas_call(
        kernel,
        out_shape=out,
        in_specs=[VMEM] * len(args) if specs is None else specs,
        out_specs=VMEM,
        scratch_shapes=list(scratch),
        compiler_params=pltpu.CompilerParams(vmem_limit_bytes=limit),
    )(*args)


def shards(traces, seg_count):
    channels, _, segments, _ = traces.shape
    rows = channels * segments
    blocks = lax.axis_size("chan")
    windows = lax.axis_size("win")
    offsets = blocks // 4
    pairs = channels * channels
    group = 2 * pairs
    forward_twiddle = jnp.asarray(twiddles(SPLIT, SPAN))
    twiddle = jnp.asarray(twiddles(RADIX, PERIOD))
    tables = jnp.asarray(np.stack(forward_tables()))
    series = traces.reshape(-1, LANES)

    own = call(
        functools.partial(whiten_kernel, rows),
        jax.ShapeDtypeStruct((rows, 2 * F), jnp.bfloat16),
        *(pltpu.with_memory_space_constraint(x, pltpu.HBM) for x in (series, tables, forward_twiddle)),
        specs=[HBM] * 3,
        scratch=(
            pltpu.VMEM(series.shape, jnp.float32),
            pltpu.VMEM(tables.shape, jnp.bfloat16),
            pltpu.VMEM(forward_twiddle.shape, jnp.float32),
            pltpu.SemaphoreType.DMA((5,)),
        ),
    )

    def to_mate(array):
        return lax.ppermute(array, "win", [(w, w ^ 1) for w in range(windows)])

    def from_block(array, offset, flip):
        moves = []
        for z in range(blocks):
            for w in range(windows):
                source = (z + offset + w % 2) % blocks * windows + (w ^ flip)
                moves.append((source, z * windows + w))
        return lax.ppermute(array, ("chan", "win"), moves)

    counts = seg_count.reshape(1, -1)
    backward = jnp.asarray(backward_table())
    own_mate = to_mate(own)
    stacks = []
    for j in range(offsets):
        visitor = from_block(own, 1 + 2 * j, 0)
        visitor_mate = from_block(own, 1 + 2 * j, 1)
        stacks.append(
            call(
                functools.partial(stack_kernel, channels, segments),
                jax.ShapeDtypeStruct((3 * group, PERIOD), jnp.float32),
                own,
                own_mate,
                visitor,
                visitor_mate,
                counts,
                backward,
                twiddle,
                scratch=(
                    pltpu.VMEM((2 * rows, 2 * F), jnp.float32),
                    pltpu.VMEM((2 * rows, 2 * F), jnp.float32),
                    pltpu.VMEM((2 * QS, 2 * PERIOD), jnp.bfloat16),
                    pltpu.VMEM((RADIX, segments * group, 2 * PERIOD), jnp.float32),
                ),
            )
        )
    stack = jnp.stack(stacks)

    step = 2
    while True:
        arrived = lax.ppermute(stack, "win", [(w, w ^ step) for w in range(windows)])
        step *= 2
        if step == windows:
            break
        stack = call(
            add_kernel, jax.ShapeDtypeStruct(stack.shape, jnp.float32), stack, arrived
        )
    result = call(
        result_kernel,
        jax.ShapeDtypeStruct((offsets, group, PERIOD), jnp.float32),
        stack,
        arrived,
        counts,
    )
    return call(
        join_kernel,
        jax.ShapeDtypeStruct((1, 2 * offsets, channels, channels, LAGS), jnp.float32),
        result,
        to_mate(result),
    )


def solution(mesh):
    placed = (P(("arrays", "chan"), "win", None, None), P("arrays"))
    return jax.shard_map(
        shards,
        mesh=mesh,
        in_specs=placed,
        out_specs=P(("arrays", "chan"), None, None, None, None),
        check_vma=False,
    )
```

```python
import functools
import math

import jax
import jax.numpy as jnp
import numpy as np
from jax import lax
from jax.experimental import pallas as pl
from jax.experimental.pallas import tpu as pltpu
from jax.sharding import PartitionSpec as P

NFFT = 2048
F = 512
LAGS = 1024
LOWEST = NFFT // 16
LANES = 128

RADIX = 4
PERIOD = NFFT // RADIX
QS = F // RADIX
SPLIT = 8
SPAN = NFFT // SPLIT
NARROW = F // SPLIT
FORWARD_Q = LOWEST // SPLIT + np.arange(NARROW)
BACKWARD_Q = np.concatenate([2 * FORWARD_Q, 2 * FORWARD_Q + 1])

VMEM = pl.BlockSpec(memory_space=pltpu.VMEM)
HBM = pl.BlockSpec(memory_space=pltpu.HBM)


def split_three(table):
    parts = []
    rest = np.asarray(table, np.float64)
    for _ in range(3):
        part = rest.astype(np.float32).astype(jnp.bfloat16)
        parts.append(part)
        rest = rest - part.astype(np.float64)
    return parts


def forward_table():
    t0 = np.arange(SPAN)
    angle = (t0[:, None] * FORWARD_Q[None, :] % SPAN) * (2 * math.pi / SPAN)
    parts = split_three(np.block([np.cos(angle), np.sin(angle)]))
    return np.concatenate(parts, axis=1)


def backward_table():
    m = np.arange(PERIOD)
    angle = (BACKWARD_Q[:, None] * m[None, :] % PERIOD) * (2 * math.pi / PERIOD)
    cosine, sine = np.cos(angle), np.sin(angle)
    halves = np.array([np.block([[cosine], [-sine]]), np.block([[sine], [cosine]])])
    table = halves.reshape(2, 2 * QS, -1, LANES).transpose(1, 2, 0, 3)
    table = table.reshape(2 * QS, 2 * PERIOD) / math.sqrt(F)
    return table.astype(np.float32).astype(jnp.bfloat16)


def twiddles(count, length):
    n = np.arange(length)
    rows = []
    for r in range(1, count):
        angle = (r * n) * (2 * math.pi / NFFT)
        rows += [np.cos(angle), np.sin(angle)]
    rows += [np.zeros(length)] * 2
    return np.stack(rows).astype(np.float32)


def eight_points(x):
    half = math.sqrt(0.5)
    s04, d04, s26, d26 = x[0] + x[4], x[0] - x[4], x[2] + x[6], x[2] - x[6]
    s15, d15, s37, d37 = x[1] + x[5], x[1] - x[5], x[3] + x[7], x[3] - x[7]
    even, odd = s04 + s26, s15 + s37
    plus, minus = (d15 + d37) * half, (d15 - d37) * half
    two = s04 - s26, s37 - s15
    one = d04 + minus, -(d26 + plus)
    three = d04 - minus, d26 - plus
    return [
        (even + odd, None),
        one,
        two,
        three,
        (even - odd, None),
        (three[0], -three[1]),
        (two[0], -two[1]),
        (one[0], -one[1]),
    ]


def whiten_kernel(
    rows,
    pairs,
    x_hbm,
    table_hbm,
    twiddle_hbm,
    count_hbm,
    backward_hbm,
    backward_twiddle_hbm,
    out_ref,
    kept_ref,
    square_ref,
    backward_ref,
    backward_twiddle_ref,
    x_ref,
    table,
    twiddle_ref,
    count_ref,
    sems,
):
    copies = [
        pltpu.make_async_copy(x_hbm, x_ref, sems.at[0]),
        pltpu.make_async_copy(twiddle_hbm, twiddle_ref, sems.at[1]),
        pltpu.make_async_copy(table_hbm, table, sems.at[2]),
        pltpu.make_async_copy(count_hbm, count_ref, sems.at[3]),
    ]
    later = [
        pltpu.make_async_copy(backward_hbm, backward_ref, sems.at[4]),
        pltpu.make_async_copy(backward_twiddle_hbm, backward_twiddle_ref, sems.at[5]),
    ]
    for copy in copies + later:
        copy.start()
    for copy in copies:
        copy.wait()

    window = lax.axis_index("win")
    mate = window + 1 - 2 * (window % 2)
    counts = count_ref[...]
    lane = lax.broadcasted_iota(jnp.int32, counts.shape, 1)
    own_count, mate_count = (
        jnp.sum(jnp.where(lane == w, counts, 0), axis=1, keepdims=True)
        for w in (window, mate)
    )
    group = 2 * pairs
    is_own = lax.broadcasted_iota(jnp.int32, (group, LANES), 0) < pairs
    count = jnp.where(is_own, own_count, mate_count)
    for k in range(kept_ref.shape[0] // group):
        kept_ref[k * group : (k + 1) * group] = (count > k).astype(jnp.float32)
    total = jnp.sum(counts, axis=1, keepdims=True).astype(jnp.float32)
    square_ref[...] = jnp.broadcast_to(total * total, square_ref.shape)

    chunks = SPAN // LANES
    real = [[] for _ in range(SPLIT)]
    imag = [[] for _ in range(SPLIT)]
    for c in range(chunks):
        x = [
            x_ref[pl.ds(t1 * chunks + c, rows, stride=SPLIT * chunks), :]
            for t1 in range(SPLIT)
        ]
        for r, (re, im) in enumerate(eight_points(x)):
            if r > 0:
                cosine, sine = (
                    twiddle_ref[2 * r - 2 + i : 2 * r - 1 + i, c * LANES : (c + 1) * LANES]
                    for i in range(2)
                )
                if im is None:
                    re, im = re * cosine, -(re * sine)
                else:
                    re, im = re * cosine + im * sine, im * cosine - re * sine
                imag[r].append(im)
            real[r].append(re)
    series = jnp.concatenate(
        [jnp.concatenate(part, axis=1) for part in real + imag[1:]], axis=0
    )
    high = series.astype(jnp.bfloat16)
    rest = series - high.astype(jnp.float32)
    mid = rest.astype(jnp.bfloat16)
    low = (rest - mid.astype(jnp.float32)).astype(jnp.bfloat16)
    dot = functools.partial(jnp.dot, preferred_element_type=jnp.float32)
    width = 2 * NARROW
    n = series.shape[0]
    both = dot(jnp.concatenate([high, mid, low], axis=0), table[:, : 2 * width])
    small = dot(high, table[:, 2 * width :])
    small = small + (both[n : 2 * n, width:] + both[2 * n :, :width])
    product = both[:n, :width] + ((both[:n, width:] + both[n : 2 * n, :width]) + small)
    left = lax.broadcasted_iota(jnp.int32, (rows, LANES), 1) < NARROW
    blocks = []
    for r in range(SPLIT):
        block = product[r * rows : (r + 1) * rows]
        block = jnp.where(left, block, -block)
        if r > 0:
            at = (SPLIT + r - 1) * rows
            block = block + pltpu.roll(product[at : at + rows], NARROW, axis=1)
        blocks.append(block)
    power = []
    for block in blocks:
        square = block * block
        power.append(square + pltpu.roll(square, NARROW, axis=1))
    total = ((power[0] + power[1]) + (power[2] + power[3])) + (
        (power[4] + power[5]) + (power[6] + power[7])
    )
    mean = jnp.sum(total, axis=1, keepdims=True) * (0.5 / F)
    floor = 0.09 * (mean + 1e-06)
    white = [b * lax.rsqrt(jnp.maximum(p, floor)) for b, p in zip(blocks, power)]
    for r in range(RADIX):
        first, second = white[r], white[r + RADIX]
        at = 2 * r * QS
        re = jnp.where(left, first, pltpu.roll(second, NARROW, axis=1))
        im = jnp.where(left, pltpu.roll(first, NARROW, axis=1), second)
        out_ref[:, at : at + QS] = re.astype(jnp.bfloat16)
        out_ref[:, at + QS : at + 2 * QS] = im.astype(jnp.bfloat16)
    for copy in later:
        copy.wait()


def stack_kernel(
    channels,
    segments,
    own_ref,
    own_mate_ref,
    visitor_ref,
    visitor_mate_ref,
    kept_ref,
    table_ref,
    twiddle_ref,
    out_ref,
    own,
    visitor,
    cross,
    inner,
):
    rows = channels * segments
    pairs = channels * channels
    group = 2 * pairs
    own[0:rows] = own_ref[...].astype(jnp.float32)
    own[rows : 2 * rows] = own_mate_ref[...].astype(jnp.float32)
    visitor[0:rows] = visitor_ref[...].astype(jnp.float32)
    visitor[rows : 2 * rows] = visitor_mate_ref[...].astype(jnp.float32)

    place = lax.broadcasted_iota(jnp.int32, (group, LANES), 0)
    own_of = place // channels
    visitor_of = place // pairs * channels + place % channels
    is_own = place < pairs

    def spread(ref, choice, segment, at):
        value = None
        for i in range(2 * channels):
            row = ref[pl.ds(i * segments + segment, 1), pl.ds(at, LANES)]
            row = jnp.broadcast_to(row, (group, LANES))
            value = row if value is None else jnp.where(choice == i, row, value)
        return value

    for r in range(RADIX):
        cross_real, cross_imag = [], []
        at = 2 * r * QS
        for k in range(segments):
            own_re = spread(own, own_of, k, at)
            own_im = spread(own, own_of, k, at + QS)
            vis_re = spread(visitor, visitor_of, k, at)
            vis_im = spread(visitor, visitor_of, k, at + QS)
            cross_real.append(own_re * vis_re + own_im * vis_im)
            cross_imag.append(own_im * vis_re - own_re * vis_im)
        at = slice(r * segments * group, (r + 1) * segments * group)
        cross[at, 0:QS] = jnp.concatenate(cross_real, axis=0).astype(jnp.bfloat16)
        cross[at, QS:] = jnp.concatenate(cross_imag, axis=0).astype(jnp.bfloat16)

    for c in range(PERIOD // LANES):
        inner[c] = jnp.dot(
            cross[...],
            table_ref[:, 2 * c * LANES : 2 * (c + 1) * LANES],
            preferred_element_type=jnp.float32,
        )

    kept = [kept_ref[k * group : (k + 1) * group] for k in range(segments)]

    for c in range(PERIOD // LANES):
        low, high = c * LANES, (c + 1) * LANES
        cos1, sin1, cos2, sin2, cos3, sin3 = (
            jnp.broadcast_to(twiddle_ref[i : i + 1, low:high], (group, LANES))
            for i in range(6)
        )
        sums = [[None] * 3, [None] * 3]
        for k in range(segments):
            re, im = (
                [
                    inner[c, pl.ds((r * segments + k) * group, group), half]
                    for r in range(RADIX)
                ]
                for half in (slice(0, LANES), slice(LANES, 2 * LANES))
            )
            re1, im1 = re[1] * cos1 - im[1] * sin1, re[1] * sin1 + im[1] * cos1
            re2, im2 = re[2] * cos2 - im[2] * sin2, re[2] * sin2 + im[2] * cos2
            re3, im3 = re[3] * cos3 - im[3] * sin3, re[3] * sin3 + im[3] * cos3
            later = (re[0] + re2) + (re1 + re3), (im[0] + im2) + (im1 + im3)
            earlier = (re[0] - re2) + (im1 - im3), (im[0] - im2) - (re1 - re3)
            for half, (direct, quadrature) in enumerate((earlier, later)):
                power = direct * direct + quadrature * quadrature
                scale = lax.rsqrt(jnp.maximum(power, 0.25)) * kept[k]
                terms = (direct * kept[k], direct * scale, quadrature * scale)
                for i, term in enumerate(terms):
                    old = sums[half][i]
                    sums[half][i] = term if old is None else old + term
        for i in range(3):
            first, second = (
                sums[half][i] + pltpu.roll(sums[half][i], pairs, axis=0)
                for half in range(2)
            )
            out_ref[i * group : (i + 1) * group, low:high] = jnp.where(
                is_own, first, second
            )


def add_kernel(left_ref, right_ref, out_ref):
    out_ref[...] = left_ref[...] + right_ref[...]


def result_kernel(left_ref, right_ref, square_ref, out_ref):
    group = out_ref.shape[1]
    for offset in range(out_ref.shape[0]):
        for low in range(0, out_ref.shape[2], LANES):
            at = slice(low, low + LANES)
            linear, cos_sum, sin_sum = (
                left_ref[offset, i * group : (i + 1) * group, at]
                + right_ref[offset, i * group : (i + 1) * group, at]
                for i in range(3)
            )
            power = cos_sum * cos_sum + sin_sum * sin_sum
            out_ref[offset, :, at] = linear * power / square_ref[...]


def join_kernel(own_ref, mate_ref, out_ref):
    core = lax.axis_index("win") % 2
    channels = out_ref.shape[2]
    half_lags = own_ref.shape[2]
    for ref, parity in ((own_ref, core), (mate_ref, 1 - core)):
        for offset in range(own_ref.shape[0]):
            for half in range(2):
                for a in range(channels):
                    row = (half * channels + a) * channels
                    lags = slice(half * half_lags, (half + 1) * half_lags)
                    out_ref[0, 2 * offset + parity, a, :, lags] = ref[
                        offset, row : row + channels
                    ]


def call(kernel, out, *args, specs=None, scratch=(), limit=8 << 20):
    return pl.pallas_call(
        kernel,
        out_shape=out,
        in_specs=[VMEM] * len(args) if specs is None else specs,
        out_specs=jax.tree.map(lambda _: VMEM, out),
        scratch_shapes=list(scratch),
        compiler_params=pltpu.CompilerParams(vmem_limit_bytes=limit),
    )(*args)


def shards(traces, seg_count):
    channels, _, segments, _ = traces.shape
    rows = channels * segments
    blocks = lax.axis_size("chan")
    windows = lax.axis_size("win")
    offsets = blocks // 4
    pairs = channels * channels
    group = 2 * pairs
    forward_twiddle = jnp.asarray(twiddles(SPLIT, SPAN))
    twiddle = jnp.asarray(twiddles(RADIX, PERIOD))
    forward = jnp.asarray(forward_table())
    series = traces.reshape(-1, LANES)

    counts = seg_count.reshape(1, -1)
    backward = jnp.asarray(backward_table())
    inputs = (series, forward, forward_twiddle, counts)
    inputs_on = (backward, twiddle)
    own, kept, square, backward, twiddle = call(
        functools.partial(whiten_kernel, rows, pairs),
        (
            jax.ShapeDtypeStruct((rows, 2 * F), jnp.bfloat16),
            jax.ShapeDtypeStruct((segments * group, LANES), jnp.float32),
            jax.ShapeDtypeStruct((group, LANES), jnp.float32),
            *(jax.ShapeDtypeStruct(x.shape, x.dtype) for x in inputs_on),
        ),
        *(pltpu.with_memory_space_constraint(x, pltpu.HBM) for x in inputs + inputs_on),
        specs=[HBM] * 6,
        scratch=(
            *(pltpu.VMEM(x.shape, x.dtype) for x in inputs),
            pltpu.SemaphoreType.DMA((6,)),
        ),
    )

    def to_mate(array):
        return lax.ppermute(array, "win", [(w, w ^ 1) for w in range(windows)])

    def from_block(array, offset, flip):
        moves = []
        for z in range(blocks):
            for w in range(windows):
                source = (z + offset + w % 2) % blocks * windows + (w ^ flip)
                moves.append((source, z * windows + w))
        return lax.ppermute(array, ("chan", "win"), moves)

    own_mate = to_mate(own)
    stacks = []
    for j in range(offsets):
        visitor = from_block(own, 1 + 2 * j, 0)
        visitor_mate = from_block(own, 1 + 2 * j, 1)
        stacks.append(
            call(
                functools.partial(stack_kernel, channels, segments),
                jax.ShapeDtypeStruct((3 * group, PERIOD), jnp.float32),
                own,
                own_mate,
                visitor,
                visitor_mate,
                kept,
                backward,
                twiddle,
                scratch=(
                    pltpu.VMEM((2 * rows, 2 * F), jnp.float32),
                    pltpu.VMEM((2 * rows, 2 * F), jnp.float32),
                    pltpu.VMEM((RADIX * segments * group, 2 * QS), jnp.bfloat16),
                    pltpu.VMEM(
                        (PERIOD // LANES, RADIX * segments * group, 2 * LANES),
                        jnp.float32,
                    ),
                ),
            )
        )
    stack = jnp.stack(stacks)

    step = 2
    while True:
        arrived = lax.ppermute(stack, "win", [(w, w ^ step) for w in range(windows)])
        step *= 2
        if step == windows:
            break
        stack = call(
            add_kernel, jax.ShapeDtypeStruct(stack.shape, jnp.float32), stack, arrived
        )
    result = call(
        result_kernel,
        jax.ShapeDtypeStruct((offsets, group, PERIOD), jnp.float32),
        stack,
        arrived,
        square,
    )
    return call(
        join_kernel,
        jax.ShapeDtypeStruct((1, 2 * offsets, channels, channels, LAGS), jnp.float32),
        result,
        to_mate(result),
    )


def solution(mesh):
    placed = (P(("arrays", "chan"), "win", None, None), P("arrays"))
    return jax.shard_map(
        shards,
        mesh=mesh,
        in_specs=placed,
        out_specs=P(("arrays", "chan"), None, None, None, None),
        check_vma=False,
    )
```

```python
import functools
import math

import jax
import jax.numpy as jnp
import numpy as np
from jax import lax
from jax.experimental import pallas as pl
from jax.experimental.pallas import tpu as pltpu
from jax.sharding import PartitionSpec as P

NFFT = 2048
F = 512
LAGS = 1024
LOWEST = NFFT // 16
LANES = 128

RADIX = 4
PERIOD = NFFT // RADIX
QS = F // RADIX
SPLIT = 8
SPAN = NFFT // SPLIT
NARROW = F // SPLIT
FORWARD_Q = LOWEST // SPLIT + np.arange(NARROW)
BACKWARD_Q = np.concatenate([2 * FORWARD_Q, 2 * FORWARD_Q + 1])

VMEM = pl.BlockSpec(memory_space=pltpu.VMEM)
HBM = pl.BlockSpec(memory_space=pltpu.HBM)


def side(block, core, blocks):
    return (core + block // (blocks // 2)) % 2


def split_three(table):
    parts = []
    rest = np.asarray(table, np.float64)
    for _ in range(3):
        part = rest.astype(np.float32).astype(jnp.bfloat16)
        parts.append(part)
        rest = rest - part.astype(np.float64)
    return parts


def forward_table():
    t0 = np.arange(SPAN)
    angle = (t0[:, None] * FORWARD_Q[None, :] % SPAN) * (2 * math.pi / SPAN)
    parts = split_three(np.block([np.cos(angle), np.sin(angle)]))
    return np.concatenate(parts, axis=1)


def backward_table():
    m = np.arange(PERIOD)
    angle = (BACKWARD_Q[:, None] * m[None, :] % PERIOD) * (2 * math.pi / PERIOD)
    cosine, sine = np.cos(angle), np.sin(angle)
    halves = np.array([np.block([[cosine], [-sine]]), np.block([[sine], [cosine]])])
    table = halves.reshape(2, 2 * QS, -1, LANES).transpose(1, 2, 0, 3)
    table = table.reshape(2 * QS, 2 * PERIOD) / math.sqrt(F)
    return table.astype(np.float32).astype(jnp.bfloat16)


def twiddles(count, length):
    n = np.arange(length)
    rows = []
    for r in range(1, count):
        angle = (r * n) * (2 * math.pi / NFFT)
        rows += [np.cos(angle), np.sin(angle)]
    rows += [np.zeros(length)] * 2
    return np.stack(rows).astype(np.float32)


def eight_points(x):
    half = math.sqrt(0.5)
    s04, d04, s26, d26 = x[0] + x[4], x[0] - x[4], x[2] + x[6], x[2] - x[6]
    s15, d15, s37, d37 = x[1] + x[5], x[1] - x[5], x[3] + x[7], x[3] - x[7]
    even, odd = s04 + s26, s15 + s37
    plus, minus = (d15 + d37) * half, (d15 - d37) * half
    two = s04 - s26, s37 - s15
    one = d04 + minus, -(d26 + plus)
    three = d04 - minus, d26 - plus
    return [
        (even + odd, None),
        one,
        two,
        three,
        (even - odd, None),
        (three[0], -three[1]),
        (two[0], -two[1]),
        (one[0], -one[1]),
    ]


def whiten_kernel(
    rows,
    pairs,
    x_hbm,
    table_hbm,
    twiddle_hbm,
    count_hbm,
    backward_hbm,
    backward_twiddle_hbm,
    out_ref,
    kept_ref,
    square_ref,
    backward_ref,
    backward_twiddle_ref,
    x_ref,
    table,
    twiddle_ref,
    count_ref,
    sems,
):
    copies = [
        pltpu.make_async_copy(x_hbm, x_ref, sems.at[0]),
        pltpu.make_async_copy(twiddle_hbm, twiddle_ref, sems.at[1]),
        pltpu.make_async_copy(table_hbm, table, sems.at[2]),
        pltpu.make_async_copy(count_hbm, count_ref, sems.at[3]),
    ]
    later = [
        pltpu.make_async_copy(backward_hbm, backward_ref, sems.at[4]),
        pltpu.make_async_copy(backward_twiddle_hbm, backward_twiddle_ref, sems.at[5]),
    ]
    for copy in copies + later:
        copy.start()
    for copy in copies:
        copy.wait()

    window = lax.axis_index("win")
    mate = window + 1 - 2 * (window % 2)
    counts = count_ref[...]
    lane = lax.broadcasted_iota(jnp.int32, counts.shape, 1)
    own_count, mate_count = (
        jnp.sum(jnp.where(lane == w, counts, 0), axis=1, keepdims=True)
        for w in (window, mate)
    )
    group = 2 * pairs
    is_own = lax.broadcasted_iota(jnp.int32, (group, LANES), 0) < pairs
    count = jnp.where(is_own, own_count, mate_count)
    for k in range(kept_ref.shape[0] // group):
        kept_ref[k * group : (k + 1) * group] = (count > k).astype(jnp.float32)
    total = jnp.sum(counts, axis=1, keepdims=True).astype(jnp.float32)
    square_ref[...] = jnp.broadcast_to(total * total, square_ref.shape)

    chunks = SPAN // LANES
    real = [[] for _ in range(SPLIT)]
    imag = [[] for _ in range(SPLIT)]
    for c in range(chunks):
        x = [
            x_ref[pl.ds(t1 * chunks + c, rows, stride=SPLIT * chunks), :]
            for t1 in range(SPLIT)
        ]
        for r, (re, im) in enumerate(eight_points(x)):
            if r > 0:
                cosine, sine = (
                    twiddle_ref[2 * r - 2 + i : 2 * r - 1 + i, c * LANES : (c + 1) * LANES]
                    for i in range(2)
                )
                if im is None:
                    re, im = re * cosine, -(re * sine)
                else:
                    re, im = re * cosine + im * sine, im * cosine - re * sine
                imag[r].append(im)
            real[r].append(re)
    series = jnp.concatenate(
        [jnp.concatenate(part, axis=1) for part in real + imag[1:]], axis=0
    )
    high = series.astype(jnp.bfloat16)
    rest = series - high.astype(jnp.float32)
    mid = rest.astype(jnp.bfloat16)
    low = (rest - mid.astype(jnp.float32)).astype(jnp.bfloat16)
    dot = functools.partial(jnp.dot, preferred_element_type=jnp.float32)
    width = 2 * NARROW
    n = series.shape[0]
    both = dot(jnp.concatenate([high, mid, low], axis=0), table[:, : 2 * width])
    small = dot(high, table[:, 2 * width :])
    small = small + (both[n : 2 * n, width:] + both[2 * n :, :width])
    product = both[:n, :width] + ((both[:n, width:] + both[n : 2 * n, :width]) + small)
    left = lax.broadcasted_iota(jnp.int32, (rows, LANES), 1) < NARROW
    blocks = []
    for r in range(SPLIT):
        block = product[r * rows : (r + 1) * rows]
        block = jnp.where(left, block, -block)
        if r > 0:
            at = (SPLIT + r - 1) * rows
            block = block + pltpu.roll(product[at : at + rows], NARROW, axis=1)
        blocks.append(block)
    power = []
    for block in blocks:
        square = block * block
        power.append(square + pltpu.roll(square, NARROW, axis=1))
    total = ((power[0] + power[1]) + (power[2] + power[3])) + (
        (power[4] + power[5]) + (power[6] + power[7])
    )
    mean = jnp.sum(total, axis=1, keepdims=True) * (0.5 / F)
    floor = 0.09 * (mean + 1e-06)
    white = [b * lax.rsqrt(jnp.maximum(p, floor)) for b, p in zip(blocks, power)]
    for r in range(RADIX):
        first, second = white[r], white[r + RADIX]
        at = 2 * r * QS
        re = jnp.where(left, first, pltpu.roll(second, NARROW, axis=1))
        im = jnp.where(left, pltpu.roll(first, NARROW, axis=1), second)
        out_ref[:, at : at + QS] = re.astype(jnp.bfloat16)
        out_ref[:, at + QS : at + 2 * QS] = im.astype(jnp.bfloat16)
    for copy in later:
        copy.wait()


def stack_kernel(
    channels,
    segments,
    own_ref,
    own_mate_ref,
    second_ref,
    first_ref,
    kept_ref,
    table_ref,
    twiddle_ref,
    out_ref,
    own,
    visitor,
    cross,
    inner,
):
    rows = channels * segments
    pairs = channels * channels
    group = 2 * pairs
    own[0:rows] = own_ref[...].astype(jnp.float32)
    own[rows : 2 * rows] = own_mate_ref[...].astype(jnp.float32)
    mine = (lax.axis_index("chan") + lax.axis_index("win")) % 2 == 0
    at = jnp.where(mine, 0, rows)
    for ref, start in ((first_ref, at), (second_ref, rows - at)):
        start = pl.multiple_of(start, 8)
        visitor[pl.ds(start, rows)] = ref[...].astype(jnp.float32)

    place = lax.broadcasted_iota(jnp.int32, (group, LANES), 0)
    own_of = place // channels
    visitor_of = place // pairs * channels + place % channels
    is_own = place < pairs

    def spread(ref, choice, segment, at):
        value = None
        for i in range(2 * channels):
            row = ref[pl.ds(i * segments + segment, 1), pl.ds(at, LANES)]
            row = jnp.broadcast_to(row, (group, LANES))
            value = row if value is None else jnp.where(choice == i, row, value)
        return value

    for r in range(RADIX):
        cross_real, cross_imag = [], []
        at = 2 * r * QS
        for k in range(segments):
            own_re = spread(own, own_of, k, at)
            own_im = spread(own, own_of, k, at + QS)
            vis_re = spread(visitor, visitor_of, k, at)
            vis_im = spread(visitor, visitor_of, k, at + QS)
            cross_real.append(own_re * vis_re + own_im * vis_im)
            cross_imag.append(own_im * vis_re - own_re * vis_im)
        at = slice(r * segments * group, (r + 1) * segments * group)
        cross[at, 0:QS] = jnp.concatenate(cross_real, axis=0).astype(jnp.bfloat16)
        cross[at, QS:] = jnp.concatenate(cross_imag, axis=0).astype(jnp.bfloat16)

    def product(c):
        inner[c] = jnp.dot(
            cross[...],
            table_ref[:, 2 * c * LANES : 2 * (c + 1) * LANES],
            preferred_element_type=jnp.float32,
        )

    product(0)
    kept = [kept_ref[k * group : (k + 1) * group] for k in range(segments)]

    for c in range(PERIOD // LANES):
        if c + 1 < PERIOD // LANES:
            product(c + 1)
        low, high = c * LANES, (c + 1) * LANES
        cos1, sin1, cos2, sin2, cos3, sin3 = (
            jnp.broadcast_to(twiddle_ref[i : i + 1, low:high], (group, LANES))
            for i in range(6)
        )
        sums = [[None] * 3, [None] * 3]
        for k in range(segments):
            re, im = (
                [
                    inner[c, pl.ds((r * segments + k) * group, group), half]
                    for r in range(RADIX)
                ]
                for half in (slice(0, LANES), slice(LANES, 2 * LANES))
            )
            re1, im1 = re[1] * cos1 - im[1] * sin1, re[1] * sin1 + im[1] * cos1
            re2, im2 = re[2] * cos2 - im[2] * sin2, re[2] * sin2 + im[2] * cos2
            re3, im3 = re[3] * cos3 - im[3] * sin3, re[3] * sin3 + im[3] * cos3
            later = (re[0] + re2) + (re1 + re3), (im[0] + im2) + (im1 + im3)
            earlier = (re[0] - re2) + (im1 - im3), (im[0] - im2) - (re1 - re3)
            for half, (direct, quadrature) in enumerate((earlier, later)):
                power = direct * direct + quadrature * quadrature
                scale = lax.rsqrt(jnp.maximum(power, 0.25)) * kept[k]
                terms = (direct * kept[k], direct * scale, quadrature * scale)
                for i, term in enumerate(terms):
                    old = sums[half][i]
                    sums[half][i] = term if old is None else old + term
        for i in range(3):
            first, second = (
                sums[half][i] + pltpu.roll(sums[half][i], pairs, axis=0)
                for half in range(2)
            )
            out_ref[i * group : (i + 1) * group, low:high] = jnp.where(
                is_own, first, second
            )


def add_kernel(left_ref, right_ref, out_ref):
    out_ref[...] = left_ref[...] + right_ref[...]


def result_kernel(left_ref, right_ref, square_ref, out_ref):
    group = out_ref.shape[1]
    for offset in range(out_ref.shape[0]):
        for low in range(0, out_ref.shape[2], LANES):
            at = slice(low, low + LANES)
            linear, cos_sum, sin_sum = (
                left_ref[offset, i * group : (i + 1) * group, at]
                + right_ref[offset, i * group : (i + 1) * group, at]
                for i in range(3)
            )
            power = cos_sum * cos_sum + sin_sum * sin_sum
            out_ref[offset, :, at] = linear * power / square_ref[...]


def join_kernel(blocks, own_ref, mate_ref, out_ref):
    parity = side(lax.axis_index("chan"), lax.axis_index("win") % 2, blocks)
    channels = out_ref.shape[2]
    half_lags = own_ref.shape[2]
    for ref, place in ((own_ref, 1 - parity), (mate_ref, parity)):
        for offset in range(own_ref.shape[0]):
            for half in range(2):
                for a in range(channels):
                    row = (half * channels + a) * channels
                    lags = slice(half * half_lags, (half + 1) * half_lags)
                    out_ref[0, 2 * offset + place, a, :, lags] = ref[
                        offset, row : row + channels
                    ]


def call(kernel, out, *args, specs=None, scratch=(), limit=8 << 20):
    return pl.pallas_call(
        kernel,
        out_shape=out,
        in_specs=[VMEM] * len(args) if specs is None else specs,
        out_specs=jax.tree.map(lambda _: VMEM, out),
        scratch_shapes=list(scratch),
        compiler_params=pltpu.CompilerParams(vmem_limit_bytes=limit),
    )(*args)


def shards(traces, seg_count):
    channels, _, segments, _ = traces.shape
    rows = channels * segments
    blocks = lax.axis_size("chan")
    windows = lax.axis_size("win")
    offsets = blocks // 4
    pairs = channels * channels
    group = 2 * pairs
    forward_twiddle = jnp.asarray(twiddles(SPLIT, SPAN))
    twiddle = jnp.asarray(twiddles(RADIX, PERIOD))
    forward = jnp.asarray(forward_table())
    series = traces.reshape(-1, LANES)

    counts = seg_count.reshape(1, -1)
    backward = jnp.asarray(backward_table())
    inputs = (series, forward, forward_twiddle, counts)
    inputs_on = (backward, twiddle)
    own, kept, square, backward, twiddle = call(
        functools.partial(whiten_kernel, rows, pairs),
        (
            jax.ShapeDtypeStruct((rows, 2 * F), jnp.bfloat16),
            jax.ShapeDtypeStruct((segments * group, LANES), jnp.float32),
            jax.ShapeDtypeStruct((group, LANES), jnp.float32),
            *(jax.ShapeDtypeStruct(x.shape, x.dtype) for x in inputs_on),
        ),
        *(pltpu.with_memory_space_constraint(x, pltpu.HBM) for x in inputs + inputs_on),
        specs=[HBM] * 6,
        scratch=(
            *(pltpu.VMEM(x.shape, x.dtype) for x in inputs),
            pltpu.SemaphoreType.DMA((6,)),
        ),
    )

    def to_mate(array):
        return lax.ppermute(array, "win", [(w, w ^ 1) for w in range(windows)])

    def from_block(array, offset, flip):
        moves = []
        for z in range(blocks):
            for w in range(windows):
                block = (z + offset + side(z, w % 2, blocks)) % blocks
                source = block * windows + w // 2 * 2 + (z % 2 ^ flip)
                moves.append((source, z * windows + w))
        return lax.ppermute(array, ("chan", "win"), moves)

    own_mate = to_mate(own)
    stacks = []
    for j in range(offsets):
        second = from_block(own, 1 + 2 * j, 1)
        first = from_block(own, 1 + 2 * j, 0)
        stacks.append(
            call(
                functools.partial(stack_kernel, channels, segments),
                jax.ShapeDtypeStruct((3 * group, PERIOD), jnp.float32),
                own,
                own_mate,
                second,
                first,
                kept,
                backward,
                twiddle,
                scratch=(
                    pltpu.VMEM((2 * rows, 2 * F), jnp.float32),
                    pltpu.VMEM((2 * rows, 2 * F), jnp.float32),
                    pltpu.VMEM((RADIX * segments * group, 2 * QS), jnp.bfloat16),
                    pltpu.VMEM(
                        (PERIOD // LANES, RADIX * segments * group, 2 * LANES),
                        jnp.float32,
                    ),
                ),
            )
        )
    stack = jnp.stack(stacks)

    def from_window(array, flip):
        return lax.ppermute(array, "win", [(w, w ^ flip) for w in range(windows)])

    for step in (1 << i for i in range(2, windows.bit_length() - 1)):
        stack = call(
            add_kernel,
            jax.ShapeDtypeStruct(stack.shape, jnp.float32),
            stack,
            from_window(stack, step),
        )
    result = call(
        result_kernel,
        jax.ShapeDtypeStruct((offsets, group, PERIOD), jnp.float32),
        from_window(stack, 1),
        from_window(stack, 3),
        square,
    )
    return call(
        functools.partial(join_kernel, blocks),
        jax.ShapeDtypeStruct((1, 2 * offsets, channels, channels, LAGS), jnp.float32),
        result,
        to_mate(result),
    )


def solution(mesh):
    placed = (P(("arrays", "chan"), "win", None, None), P("arrays"))
    return jax.shard_map(
        shards,
        mesh=mesh,
        in_specs=placed,
        out_specs=P(("arrays", "chan"), None, None, None, None),
        check_vma=False,
    )
```

```python
import functools
import math

import jax
import jax.numpy as jnp
import numpy as np
from jax import lax
from jax.experimental import pallas as pl
from jax.experimental.pallas import tpu as pltpu
from jax.sharding import PartitionSpec as P

NFFT = 2048
F = 512
LAGS = 1024
LOWEST = NFFT // 16
LANES = 128

RADIX = 4
PERIOD = NFFT // RADIX
QS = F // RADIX
SPLIT = 8
SPAN = NFFT // SPLIT
NARROW = F // SPLIT
FORWARD_Q = LOWEST // SPLIT + np.arange(NARROW)
BACKWARD_Q = np.concatenate([2 * FORWARD_Q, 2 * FORWARD_Q + 1])

VMEM = pl.BlockSpec(memory_space=pltpu.VMEM)
HBM = pl.BlockSpec(memory_space=pltpu.HBM)


def side(block, core, blocks):
    return (core + block // (blocks // 2)) % 2


def split_three(table):
    parts = []
    rest = np.asarray(table, np.float64)
    for _ in range(3):
        part = rest.astype(np.float32).astype(jnp.bfloat16)
        parts.append(part)
        rest = rest - part.astype(np.float64)
    return parts


def forward_table():
    t0 = np.arange(SPAN)
    angle = (t0[:, None] * FORWARD_Q[None, :] % SPAN) * (2 * math.pi / SPAN)
    parts = split_three(np.block([np.cos(angle), np.sin(angle)]))
    return np.concatenate(parts, axis=1)


def backward_table():
    m = np.arange(PERIOD)
    angle = (BACKWARD_Q[:, None] * m[None, :] % PERIOD) * (2 * math.pi / PERIOD)
    cosine, sine = np.cos(angle), np.sin(angle)
    halves = np.array([np.block([[cosine], [-sine]]), np.block([[sine], [cosine]])])
    table = halves.reshape(2, 2 * QS, -1, LANES).transpose(1, 2, 0, 3)
    table = table.reshape(2 * QS, 2 * PERIOD) / math.sqrt(F)
    return table.astype(np.float32).astype(jnp.bfloat16)


def twiddles(count, length):
    n = np.arange(length)
    rows = []
    for r in range(1, count):
        angle = (r * n) * (2 * math.pi / NFFT)
        rows += [np.cos(angle), np.sin(angle)]
    rows += [np.zeros(length)] * 2
    return np.stack(rows).astype(np.float32)


def eight_points(x):
    half = math.sqrt(0.5)
    s04, d04, s26, d26 = x[0] + x[4], x[0] - x[4], x[2] + x[6], x[2] - x[6]
    s15, d15, s37, d37 = x[1] + x[5], x[1] - x[5], x[3] + x[7], x[3] - x[7]
    even, odd = s04 + s26, s15 + s37
    plus, minus = (d15 + d37) * half, (d15 - d37) * half
    two = s04 - s26, s37 - s15
    one = d04 + minus, -(d26 + plus)
    three = d04 - minus, d26 - plus
    return [
        (even + odd, None),
        one,
        two,
        three,
        (even - odd, None),
        (three[0], -three[1]),
        (two[0], -two[1]),
        (one[0], -one[1]),
    ]


def whiten_kernel(
    rows,
    pairs,
    x_hbm,
    table_hbm,
    twiddle_hbm,
    count_hbm,
    backward_hbm,
    backward_twiddle_hbm,
    out_ref,
    kept_ref,
    square_ref,
    backward_ref,
    backward_twiddle_ref,
    x_ref,
    table,
    twiddle_ref,
    count_ref,
    sems,
):
    copies = [
        pltpu.make_async_copy(twiddle_hbm, twiddle_ref, sems.at[1]),
        pltpu.make_async_copy(table_hbm, table, sems.at[2]),
        pltpu.make_async_copy(count_hbm, count_ref, sems.at[3]),
    ]
    piece = x_ref.shape[0] // 4
    for i in range(4):
        at = pl.ds(i * piece, piece)
        copies.append(
            pltpu.make_async_copy(x_hbm.at[at], x_ref.at[at], sems.at[6 + i])
        )
    later = [
        pltpu.make_async_copy(backward_hbm, backward_ref, sems.at[4]),
        pltpu.make_async_copy(backward_twiddle_hbm, backward_twiddle_ref, sems.at[5]),
    ]
    for copy in copies + later:
        copy.start()
    for copy in copies:
        copy.wait()

    window = lax.axis_index("win")
    mate = window + 1 - 2 * (window % 2)
    counts = count_ref[...]
    lane = lax.broadcasted_iota(jnp.int32, counts.shape, 1)
    own_count, mate_count = (
        jnp.sum(jnp.where(lane == w, counts, 0), axis=1, keepdims=True)
        for w in (window, mate)
    )
    group = 2 * pairs
    is_own = lax.broadcasted_iota(jnp.int32, (group, LANES), 0) < pairs
    count = jnp.where(is_own, own_count, mate_count)
    for k in range(kept_ref.shape[0] // group):
        kept_ref[k * group : (k + 1) * group] = (count > k).astype(jnp.float32)
    total = jnp.sum(counts, axis=1, keepdims=True).astype(jnp.float32)
    square_ref[...] = jnp.broadcast_to(total * total, square_ref.shape)

    chunks = SPAN // LANES
    real = [[] for _ in range(SPLIT)]
    imag = [[] for _ in range(SPLIT)]
    for c in range(chunks):
        x = [
            x_ref[pl.ds(t1 * chunks + c, rows, stride=SPLIT * chunks), :]
            for t1 in range(SPLIT)
        ]
        for r, (re, im) in enumerate(eight_points(x)):
            if r > 0:
                cosine, sine = (
                    twiddle_ref[2 * r - 2 + i : 2 * r - 1 + i, c * LANES : (c + 1) * LANES]
                    for i in range(2)
                )
                if im is None:
                    re, im = re * cosine, -(re * sine)
                else:
                    re, im = re * cosine + im * sine, im * cosine - re * sine
                imag[r].append(im)
            real[r].append(re)
    series = jnp.concatenate(
        [jnp.concatenate(part, axis=1) for part in real + imag[1:]], axis=0
    )
    high = series.astype(jnp.bfloat16)
    rest = series - high.astype(jnp.float32)
    mid = rest.astype(jnp.bfloat16)
    low = (rest - mid.astype(jnp.float32)).astype(jnp.bfloat16)
    dot = functools.partial(jnp.dot, preferred_element_type=jnp.float32)
    width = 2 * NARROW
    n = series.shape[0]
    both = dot(jnp.concatenate([high, mid, low], axis=0), table[:, : 2 * width])
    small = dot(high, table[:, 2 * width :])
    small = small + (both[n : 2 * n, width:] + both[2 * n :, :width])
    product = both[:n, :width] + ((both[:n, width:] + both[n : 2 * n, :width]) + small)
    left = lax.broadcasted_iota(jnp.int32, (rows, LANES), 1) < NARROW
    blocks = []
    for r in range(SPLIT):
        block = product[r * rows : (r + 1) * rows]
        block = jnp.where(left, block, -block)
        if r > 0:
            at = (SPLIT + r - 1) * rows
            block = block + pltpu.roll(product[at : at + rows], NARROW, axis=1)
        blocks.append(block)
    power = []
    for block in blocks:
        square = block * block
        power.append(square + pltpu.roll(square, NARROW, axis=1))
    total = ((power[0] + power[1]) + (power[2] + power[3])) + (
        (power[4] + power[5]) + (power[6] + power[7])
    )
    mean = jnp.sum(total, axis=1, keepdims=True) * (0.5 / F)
    most = lax.rsqrt(0.09 * (mean + 1e-06))
    white = [
        b * jnp.minimum(lax.rsqrt(jnp.maximum(p, 1e-08)), most)
        for b, p in zip(blocks, power)
    ]
    for r in range(RADIX):
        first, second = white[r], white[r + RADIX]
        at = 2 * r * QS
        re = jnp.where(left, first, pltpu.roll(second, NARROW, axis=1))
        im = jnp.where(left, pltpu.roll(first, NARROW, axis=1), second)
        out_ref[:, at : at + QS] = re.astype(jnp.bfloat16)
        out_ref[:, at + QS : at + 2 * QS] = im.astype(jnp.bfloat16)
    for copy in later:
        copy.wait()


def stack_kernel(
    channels,
    segments,
    own_ref,
    own_mate_ref,
    second_ref,
    first_ref,
    kept_ref,
    table_ref,
    twiddle_ref,
    out_ref,
    own,
    visitor,
    cross,
    inner,
):
    rows = channels * segments
    pairs = channels * channels
    group = 2 * pairs
    own[0:rows] = own_ref[...].astype(jnp.float32)
    own[rows : 2 * rows] = own_mate_ref[...].astype(jnp.float32)
    mine = (lax.axis_index("chan") + lax.axis_index("win")) % 2 == 0
    at = jnp.where(mine, 0, rows)
    for ref, start in ((first_ref, at), (second_ref, rows - at)):
        start = pl.multiple_of(start, 8)
        visitor[pl.ds(start, rows)] = ref[...].astype(jnp.float32)

    place = lax.broadcasted_iota(jnp.int32, (group, LANES), 0)
    own_of = place // channels
    visitor_of = place // pairs * channels + place % channels
    is_own = place < pairs

    def spread(ref, choice, segment, at):
        value = None
        for i in range(2 * channels):
            row = ref[pl.ds(i * segments + segment, 1), pl.ds(at, LANES)]
            row = jnp.broadcast_to(row, (group, LANES))
            value = row if value is None else jnp.where(choice == i, row, value)
        return value

    kept = [kept_ref[k * group : (k + 1) * group] for k in range(segments)]

    for r in range(RADIX):
        cross_real, cross_imag = [], []
        at = 2 * r * QS
        for k in range(segments):
            own_re = spread(own, own_of, k, at)
            own_im = spread(own, own_of, k, at + QS)
            vis_re = spread(visitor, visitor_of, k, at)
            vis_im = spread(visitor, visitor_of, k, at + QS)
            vis_re, vis_im = vis_re * kept[k], vis_im * kept[k]
            cross_real.append(own_re * vis_re + own_im * vis_im)
            cross_imag.append(own_im * vis_re - own_re * vis_im)
        at = slice(r * segments * group, (r + 1) * segments * group)
        cross[at, 0:QS] = jnp.concatenate(cross_real, axis=0).astype(jnp.bfloat16)
        cross[at, QS:] = jnp.concatenate(cross_imag, axis=0).astype(jnp.bfloat16)

    def product(c):
        inner[c] = jnp.dot(
            cross[...],
            table_ref[:, 2 * c * LANES : 2 * (c + 1) * LANES],
            preferred_element_type=jnp.float32,
        )

    product(0)
    for c in range(PERIOD // LANES):
        if c + 1 < PERIOD // LANES:
            product(c + 1)
        low, high = c * LANES, (c + 1) * LANES
        cos1, sin1, cos2, sin2, cos3, sin3 = (
            jnp.broadcast_to(twiddle_ref[i : i + 1, low:high], (group, LANES))
            for i in range(6)
        )
        sums = [[None] * 3, [None] * 3]
        for k in range(segments):
            re, im = (
                [
                    inner[c, pl.ds((r * segments + k) * group, group), half]
                    for r in range(RADIX)
                ]
                for half in (slice(0, LANES), slice(LANES, 2 * LANES))
            )
            re1, im1 = re[1] * cos1 - im[1] * sin1, re[1] * sin1 + im[1] * cos1
            re2, im2 = re[2] * cos2 - im[2] * sin2, re[2] * sin2 + im[2] * cos2
            re3, im3 = re[3] * cos3 - im[3] * sin3, re[3] * sin3 + im[3] * cos3
            later = (re[0] + re2) + (re1 + re3), (im[0] + im2) + (im1 + im3)
            earlier = (re[0] - re2) + (im1 - im3), (im[0] - im2) - (re1 - re3)
            for half, (direct, quadrature) in enumerate((earlier, later)):
                power = direct * direct + quadrature * quadrature
                scale = lax.rsqrt(jnp.maximum(power, 0.25))
                terms = (direct, direct * scale, quadrature * scale)
                for i, term in enumerate(terms):
                    old = sums[half][i]
                    sums[half][i] = term if old is None else old + term
        for i in range(3):
            first, second = (
                sums[half][i] + pltpu.roll(sums[half][i], pairs, axis=0)
                for half in range(2)
            )
            out_ref[i * group : (i + 1) * group, low:high] = jnp.where(
                is_own, first, second
            )


def add_kernel(left_ref, right_ref, out_ref):
    out_ref[...] = left_ref[...] + right_ref[...]


def result_kernel(left_ref, right_ref, square_ref, out_ref):
    group = out_ref.shape[1]
    for offset in range(out_ref.shape[0]):
        for low in range(0, out_ref.shape[2], LANES):
            at = slice(low, low + LANES)
            linear, cos_sum, sin_sum = (
                left_ref[offset, i * group : (i + 1) * group, at]
                + right_ref[offset, i * group : (i + 1) * group, at]
                for i in range(3)
            )
            power = cos_sum * cos_sum + sin_sum * sin_sum
            out_ref[offset, :, at] = linear * power / square_ref[...]


def join_kernel(blocks, own_ref, mate_ref, out_ref):
    parity = side(lax.axis_index("chan"), lax.axis_index("win") % 2, blocks)
    channels = out_ref.shape[2]
    half_lags = own_ref.shape[2]
    for ref, place in ((own_ref, 1 - parity), (mate_ref, parity)):
        for offset in range(own_ref.shape[0]):
            for half in range(2):
                for a in range(channels):
                    row = (half * channels + a) * channels
                    lags = slice(half * half_lags, (half + 1) * half_lags)
                    out_ref[0, 2 * offset + place, a, :, lags] = ref[
                        offset, row : row + channels
                    ]


def call(kernel, out, *args, specs=None, scratch=(), limit=8 << 20):
    return pl.pallas_call(
        kernel,
        out_shape=out,
        in_specs=[VMEM] * len(args) if specs is None else specs,
        out_specs=jax.tree.map(lambda _: VMEM, out),
        scratch_shapes=list(scratch),
        compiler_params=pltpu.CompilerParams(vmem_limit_bytes=limit),
    )(*args)


def shards(traces, seg_count):
    channels, _, segments, _ = traces.shape
    rows = channels * segments
    blocks = lax.axis_size("chan")
    windows = lax.axis_size("win")
    offsets = blocks // 4
    pairs = channels * channels
    group = 2 * pairs
    forward_twiddle = jnp.asarray(twiddles(SPLIT, SPAN))
    twiddle = jnp.asarray(twiddles(RADIX, PERIOD))
    forward = jnp.asarray(forward_table())
    series = traces.reshape(-1, LANES)

    counts = seg_count.reshape(1, -1)
    backward = jnp.asarray(backward_table())
    inputs = (series, forward, forward_twiddle, counts)
    inputs_on = (backward, twiddle)
    own, kept, square, backward, twiddle = call(
        functools.partial(whiten_kernel, rows, pairs),
        (
            jax.ShapeDtypeStruct((rows, 2 * F), jnp.bfloat16),
            jax.ShapeDtypeStruct((segments * group, LANES), jnp.float32),
            jax.ShapeDtypeStruct((group, LANES), jnp.float32),
            *(jax.ShapeDtypeStruct(x.shape, x.dtype) for x in inputs_on),
        ),
        *(pltpu.with_memory_space_constraint(x, pltpu.HBM) for x in inputs + inputs_on),
        specs=[HBM] * 6,
        scratch=(
            *(pltpu.VMEM(x.shape, x.dtype) for x in inputs),
            pltpu.SemaphoreType.DMA((10,)),
        ),
    )

    def to_mate(array):
        return lax.ppermute(array, "win", [(w, w ^ 1) for w in range(windows)])

    def from_block(array, offset, flip):
        moves = []
        for z in range(blocks):
            for w in range(windows):
                block = (z + offset + side(z, w % 2, blocks)) % blocks
                source = block * windows + w // 2 * 2 + (z % 2 ^ flip)
                moves.append((source, z * windows + w))
        return lax.ppermute(array, ("chan", "win"), moves)

    own_mate = to_mate(own)
    stacks = []
    for j in range(offsets):
        second = from_block(own, 1 + 2 * j, 1)
        first = from_block(own, 1 + 2 * j, 0)
        stacks.append(
            call(
                functools.partial(stack_kernel, channels, segments),
                jax.ShapeDtypeStruct((3 * group, PERIOD), jnp.float32),
                own,
                own_mate,
                second,
                first,
                kept,
                backward,
                twiddle,
                scratch=(
                    pltpu.VMEM((2 * rows, 2 * F), jnp.float32),
                    pltpu.VMEM((2 * rows, 2 * F), jnp.float32),
                    pltpu.VMEM((RADIX * segments * group, 2 * QS), jnp.bfloat16),
                    pltpu.VMEM(
                        (PERIOD // LANES, RADIX * segments * group, 2 * LANES),
                        jnp.float32,
                    ),
                ),
            )
        )
    stack = jnp.stack(stacks)

    def from_window(array, flip):
        return lax.ppermute(array, "win", [(w, w ^ flip) for w in range(windows)])

    for step in (1 << i for i in range(2, windows.bit_length() - 1)):
        stack = call(
            add_kernel,
            jax.ShapeDtypeStruct(stack.shape, jnp.float32),
            stack,
            from_window(stack, step),
        )
    result = call(
        result_kernel,
        jax.ShapeDtypeStruct((offsets, group, PERIOD), jnp.float32),
        from_window(stack, 1),
        from_window(stack, 3),
        square,
    )
    return call(
        functools.partial(join_kernel, blocks),
        jax.ShapeDtypeStruct((1, 2 * offsets, channels, channels, LAGS), jnp.float32),
        result,
        to_mate(result),
    )


def solution(mesh):
    placed = (P(("arrays", "chan"), "win", None, None), P("arrays"))
    return jax.shard_map(
        shards,
        mesh=mesh,
        in_specs=placed,
        out_specs=P(("arrays", "chan"), None, None, None, None),
        check_vma=False,
    )
```

```python
import functools
import math

import jax
import jax.numpy as jnp
import numpy as np
from jax import lax
from jax.experimental import pallas as pl
from jax.experimental.pallas import tpu as pltpu
from jax.sharding import PartitionSpec as P

NFFT = 2048
F = 512
LAGS = 1024
LOWEST = NFFT // 16
LANES = 128

RADIX = 4
PERIOD = NFFT // RADIX
QS = F // RADIX
SPLIT = 8
SPAN = NFFT // SPLIT
NARROW = F // SPLIT
FORWARD_Q = LOWEST // SPLIT + np.arange(NARROW)
BACKWARD_Q = np.concatenate([2 * FORWARD_Q, 2 * FORWARD_Q + 1])

VMEM = pl.BlockSpec(memory_space=pltpu.VMEM)
HBM = pl.BlockSpec(memory_space=pltpu.HBM)


def side(block, core, blocks):
    return (core + block // (blocks // 2)) % 2


def split_three(table):
    parts = []
    rest = np.asarray(table, np.float64)
    for _ in range(3):
        part = rest.astype(np.float32).astype(jnp.bfloat16)
        parts.append(part)
        rest = rest - part.astype(np.float64)
    return parts


def forward_table():
    t0 = np.arange(SPAN)
    angle = (t0[:, None] * FORWARD_Q[None, :] % SPAN) * (2 * math.pi / SPAN)
    parts = split_three(np.block([np.cos(angle), np.sin(angle)]))
    return np.concatenate(parts, axis=1)


def backward_table():
    m = np.arange(PERIOD)
    angle = (BACKWARD_Q[:, None] * m[None, :] % PERIOD) * (2 * math.pi / PERIOD)
    cosine, sine = np.cos(angle), np.sin(angle)
    halves = np.array([np.block([[cosine], [-sine]]), np.block([[sine], [cosine]])])
    table = halves.reshape(2, 2 * QS, -1, LANES).transpose(1, 2, 0, 3)
    table = table.reshape(2 * QS, 2 * PERIOD) / math.sqrt(F)
    return table.astype(np.float32).astype(jnp.bfloat16)


def twiddles(count, length):
    n = np.arange(length)
    rows = []
    for r in range(1, count):
        angle = (r * n) * (2 * math.pi / NFFT)
        rows += [np.cos(angle), np.sin(angle)]
    rows += [np.zeros(length)] * 2
    return np.stack(rows).astype(np.float32)


def eight_points(x):
    half = math.sqrt(0.5)
    s04, d04, s26, d26 = x[0] + x[4], x[0] - x[4], x[2] + x[6], x[2] - x[6]
    s15, d15, s37, d37 = x[1] + x[5], x[1] - x[5], x[3] + x[7], x[3] - x[7]
    even, odd = s04 + s26, s15 + s37
    plus, minus = (d15 + d37) * half, (d15 - d37) * half
    two = s04 - s26, s37 - s15
    one = d04 + minus, -(d26 + plus)
    three = d04 - minus, d26 - plus
    return [
        (even + odd, None),
        one,
        two,
        three,
        (even - odd, None),
        (three[0], -three[1]),
        (two[0], -two[1]),
        (one[0], -one[1]),
    ]


def whiten_kernel(
    rows,
    pairs,
    x_hbm,
    table_hbm,
    twiddle_hbm,
    count_hbm,
    backward_hbm,
    backward_twiddle_hbm,
    out_ref,
    kept_ref,
    square_ref,
    backward_ref,
    backward_twiddle_ref,
    x_ref,
    table,
    twiddle_ref,
    count_ref,
    sems,
):
    copies = [
        pltpu.make_async_copy(twiddle_hbm, twiddle_ref, sems.at[1]),
        pltpu.make_async_copy(table_hbm, table, sems.at[2]),
        pltpu.make_async_copy(count_hbm, count_ref, sems.at[3]),
    ]
    piece = x_ref.shape[0] // 4
    for i in range(4):
        at = pl.ds(i * piece, piece)
        copies.append(
            pltpu.make_async_copy(x_hbm.at[at], x_ref.at[at], sems.at[6 + i])
        )
    later = [
        pltpu.make_async_copy(backward_hbm, backward_ref, sems.at[4]),
        pltpu.make_async_copy(backward_twiddle_hbm, backward_twiddle_ref, sems.at[5]),
    ]
    for copy in copies + later:
        copy.start()
    for copy in copies:
        copy.wait()

    window = lax.axis_index("win")
    mate = window + 1 - 2 * (window % 2)
    counts = count_ref[...]
    lane = lax.broadcasted_iota(jnp.int32, counts.shape, 1)
    own_count, mate_count = (
        jnp.sum(jnp.where(lane == w, counts, 0), axis=1, keepdims=True)
        for w in (window, mate)
    )
    group = 2 * pairs
    is_own = lax.broadcasted_iota(jnp.int32, (group, LANES), 0) < pairs
    count = jnp.where(is_own, own_count, mate_count)
    for k in range(kept_ref.shape[0] // group):
        kept_ref[k * group : (k + 1) * group] = (count > k).astype(jnp.float32)
    total = jnp.sum(counts, axis=1, keepdims=True).astype(jnp.float32)
    square_ref[...] = jnp.broadcast_to(total * total, square_ref.shape)

    chunks = SPAN // LANES
    real = [[] for _ in range(SPLIT)]
    imag = [[] for _ in range(SPLIT)]
    for c in range(chunks):
        x = [
            x_ref[pl.ds(t1 * chunks + c, rows, stride=SPLIT * chunks), :]
            for t1 in range(SPLIT)
        ]
        for r, (re, im) in enumerate(eight_points(x)):
            if r > 0:
                cosine, sine = (
                    twiddle_ref[2 * r - 2 + i : 2 * r - 1 + i, c * LANES : (c + 1) * LANES]
                    for i in range(2)
                )
                if im is None:
                    re, im = re * cosine, -(re * sine)
                else:
                    re, im = re * cosine + im * sine, im * cosine - re * sine
                imag[r].append(im)
            real[r].append(re)
    series = jnp.concatenate(
        [jnp.concatenate(part, axis=1) for part in real + imag[1:]], axis=0
    )
    high = series.astype(jnp.bfloat16)
    rest = series - high.astype(jnp.float32)
    mid = rest.astype(jnp.bfloat16)
    low = (rest - mid.astype(jnp.float32)).astype(jnp.bfloat16)
    dot = functools.partial(jnp.dot, preferred_element_type=jnp.float32)
    width = 2 * NARROW
    n = series.shape[0]
    both = dot(jnp.concatenate([high, mid, low], axis=0), table[:, : 2 * width])
    small = dot(high, table[:, 2 * width :])
    small = small + (both[n : 2 * n, width:] + both[2 * n :, :width])
    product = both[:n, :width] + ((both[:n, width:] + both[n : 2 * n, :width]) + small)
    left = lax.broadcasted_iota(jnp.int32, (rows, LANES), 1) < NARROW
    blocks = []
    for r in range(SPLIT):
        block = product[r * rows : (r + 1) * rows]
        block = jnp.where(left, block, -block)
        if r > 0:
            at = (SPLIT + r - 1) * rows
            block = block + pltpu.roll(product[at : at + rows], NARROW, axis=1)
        blocks.append(block)
    power = []
    for block in blocks:
        square = block * block
        power.append(square + pltpu.roll(square, NARROW, axis=1))
    total = ((power[0] + power[1]) + (power[2] + power[3])) + (
        (power[4] + power[5]) + (power[6] + power[7])
    )
    mean = jnp.sum(total, axis=1, keepdims=True) * (0.5 / F)
    most = lax.rsqrt(0.09 * (mean + 1e-06))
    white = [
        b * jnp.minimum(lax.rsqrt(jnp.maximum(p, 1e-08)), most)
        for b, p in zip(blocks, power)
    ]
    for r in range(RADIX):
        first, second = white[r], white[r + RADIX]
        at = 2 * r * QS
        re = jnp.where(left, first, pltpu.roll(second, NARROW, axis=1))
        im = jnp.where(left, pltpu.roll(first, NARROW, axis=1), second)
        out_ref[:, at : at + QS] = re.astype(jnp.bfloat16)
        out_ref[:, at + QS : at + 2 * QS] = im.astype(jnp.bfloat16)
    for copy in later:
        copy.wait()


def stack_kernel(
    channels,
    segments,
    own_ref,
    own_mate_ref,
    second_ref,
    first_ref,
    kept_ref,
    table_ref,
    twiddle_ref,
    out_ref,
    own,
    visitor,
    cross,
    inner,
):
    rows = channels * segments
    pairs = channels * channels
    group = 2 * pairs
    own[0:rows] = own_ref[...].astype(jnp.float32)
    own[rows : 2 * rows] = own_mate_ref[...].astype(jnp.float32)
    mine = (lax.axis_index("chan") + lax.axis_index("win")) % 2 == 0
    at = jnp.where(mine, 0, rows)
    for ref, start in ((first_ref, at), (second_ref, rows - at)):
        start = pl.multiple_of(start, 8)
        visitor[pl.ds(start, rows)] = ref[...].astype(jnp.float32)

    place = lax.broadcasted_iota(jnp.int32, (group, LANES), 0)
    own_of = place // channels
    visitor_of = place // pairs * channels + place % channels
    is_own = place < pairs

    def spread(ref, choice, segment, at):
        value = None
        for i in range(2 * channels):
            row = ref[pl.ds(i * segments + segment, 1), pl.ds(at, LANES)]
            row = jnp.broadcast_to(row, (group, LANES))
            value = row if value is None else jnp.where(choice == i, row, value)
        return value

    kept = [kept_ref[k * group : (k + 1) * group] for k in range(segments)]

    for r in range(RADIX):
        cross_real, cross_imag = [], []
        at = 2 * r * QS
        for k in range(segments):
            own_re = spread(own, own_of, k, at)
            own_im = spread(own, own_of, k, at + QS)
            vis_re = spread(visitor, visitor_of, k, at)
            vis_im = spread(visitor, visitor_of, k, at + QS)
            vis_re, vis_im = vis_re * kept[k], vis_im * kept[k]
            cross_real.append(own_re * vis_re + own_im * vis_im)
            cross_imag.append(own_im * vis_re - own_re * vis_im)
        at = slice(r * segments * group, (r + 1) * segments * group)
        cross[at, 0:QS] = jnp.concatenate(cross_real, axis=0).astype(jnp.bfloat16)
        cross[at, QS:] = jnp.concatenate(cross_imag, axis=0).astype(jnp.bfloat16)
        inner[0, at] = jnp.dot(
            cross[at],
            table_ref[:, : 2 * LANES],
            preferred_element_type=jnp.float32,
        )

    def product(c):
        inner[c] = jnp.dot(
            cross[...],
            table_ref[:, 2 * c * LANES : 2 * (c + 1) * LANES],
            preferred_element_type=jnp.float32,
        )

    for c in range(PERIOD // LANES):
        if c + 1 < PERIOD // LANES:
            product(c + 1)
        low, high = c * LANES, (c + 1) * LANES
        cos1, sin1, cos2, sin2, cos3, sin3 = (
            jnp.broadcast_to(twiddle_ref[i : i + 1, low:high], (group, LANES))
            for i in range(6)
        )
        sums = [[None] * 3, [None] * 3]
        for k in range(segments):
            re, im = (
                [
                    inner[c, pl.ds((r * segments + k) * group, group), half]
                    for r in range(RADIX)
                ]
                for half in (slice(0, LANES), slice(LANES, 2 * LANES))
            )
            re1, im1 = re[1] * cos1 - im[1] * sin1, re[1] * sin1 + im[1] * cos1
            re2, im2 = re[2] * cos2 - im[2] * sin2, re[2] * sin2 + im[2] * cos2
            re3, im3 = re[3] * cos3 - im[3] * sin3, re[3] * sin3 + im[3] * cos3
            later = (re[0] + re2) + (re1 + re3), (im[0] + im2) + (im1 + im3)
            earlier = (re[0] - re2) + (im1 - im3), (im[0] - im2) - (re1 - re3)
            for half, (direct, quadrature) in enumerate((earlier, later)):
                power = direct * direct + quadrature * quadrature
                scale = lax.rsqrt(jnp.maximum(power, 0.25))
                terms = (direct, direct * scale, quadrature * scale)
                for i, term in enumerate(terms):
                    old = sums[half][i]
                    sums[half][i] = term if old is None else old + term
        for i in range(3):
            first, second = (
                sums[half][i] + pltpu.roll(sums[half][i], pairs, axis=0)
                for half in range(2)
            )
            out_ref[i * group : (i + 1) * group, low:high] = jnp.where(
                is_own, first, second
            )


def add_kernel(left_ref, right_ref, out_ref):
    out_ref[...] = left_ref[...] + right_ref[...]


def result_kernel(left_ref, right_ref, square_ref, out_ref):
    group = out_ref.shape[1]
    for offset in range(out_ref.shape[0]):
        for low in range(0, out_ref.shape[2], LANES):
            at = slice(low, low + LANES)
            linear, cos_sum, sin_sum = (
                left_ref[offset, i * group : (i + 1) * group, at]
                + right_ref[offset, i * group : (i + 1) * group, at]
                for i in range(3)
            )
            power = cos_sum * cos_sum + sin_sum * sin_sum
            out_ref[offset, :, at] = linear * power / square_ref[...]


def join_kernel(blocks, own_ref, mate_ref, out_ref):
    parity = side(lax.axis_index("chan"), lax.axis_index("win") % 2, blocks)
    channels = out_ref.shape[2]
    half_lags = own_ref.shape[2]
    for ref, place in ((own_ref, 1 - parity), (mate_ref, parity)):
        for offset in range(own_ref.shape[0]):
            for half in range(2):
                for a in range(channels):
                    row = (half * channels + a) * channels
                    lags = slice(half * half_lags, (half + 1) * half_lags)
                    out_ref[0, 2 * offset + place, a, :, lags] = ref[
                        offset, row : row + channels
                    ]


def call(kernel, out, *args, specs=None, scratch=(), limit=8 << 20):
    return pl.pallas_call(
        kernel,
        out_shape=out,
        in_specs=[VMEM] * len(args) if specs is None else specs,
        out_specs=jax.tree.map(lambda _: VMEM, out),
        scratch_shapes=list(scratch),
        compiler_params=pltpu.CompilerParams(vmem_limit_bytes=limit),
    )(*args)


def shards(traces, seg_count):
    channels, _, segments, _ = traces.shape
    rows = channels * segments
    blocks = lax.axis_size("chan")
    windows = lax.axis_size("win")
    offsets = blocks // 4
    pairs = channels * channels
    group = 2 * pairs
    forward_twiddle = jnp.asarray(twiddles(SPLIT, SPAN))
    twiddle = jnp.asarray(twiddles(RADIX, PERIOD))
    forward = jnp.asarray(forward_table())
    series = traces.reshape(-1, LANES)

    counts = seg_count.reshape(1, -1)
    backward = jnp.asarray(backward_table())
    inputs = (series, forward, forward_twiddle, counts)
    inputs_on = (backward, twiddle)
    own, kept, square, backward, twiddle = call(
        functools.partial(whiten_kernel, rows, pairs),
        (
            jax.ShapeDtypeStruct((rows, 2 * F), jnp.bfloat16),
            jax.ShapeDtypeStruct((segments * group, LANES), jnp.float32),
            jax.ShapeDtypeStruct((group, LANES), jnp.float32),
            *(jax.ShapeDtypeStruct(x.shape, x.dtype) for x in inputs_on),
        ),
        *(pltpu.with_memory_space_constraint(x, pltpu.HBM) for x in inputs + inputs_on),
        specs=[HBM] * 6,
        scratch=(
            *(pltpu.VMEM(x.shape, x.dtype) for x in inputs),
            pltpu.SemaphoreType.DMA((10,)),
        ),
    )

    def to_mate(array):
        return lax.ppermute(array, "win", [(w, w ^ 1) for w in range(windows)])

    def from_block(array, offset, flip):
        moves = []
        for z in range(blocks):
            for w in range(windows):
                block = (z + offset + side(z, w % 2, blocks)) % blocks
                source = block * windows + w // 2 * 2 + (z % 2 ^ flip)
                moves.append((source, z * windows + w))
        return lax.ppermute(array, ("chan", "win"), moves)

    own_mate = to_mate(own)
    stacks = []
    for j in range(offsets):
        second = from_block(own, 1 + 2 * j, 1)
        first = from_block(own, 1 + 2 * j, 0)
        stacks.append(
            call(
                functools.partial(stack_kernel, channels, segments),
                jax.ShapeDtypeStruct((3 * group, PERIOD), jnp.float32),
                own,
                own_mate,
                second,
                first,
                kept,
                backward,
                twiddle,
                scratch=(
                    pltpu.VMEM((2 * rows, 2 * F), jnp.float32),
                    pltpu.VMEM((2 * rows, 2 * F), jnp.float32),
                    pltpu.VMEM((RADIX * segments * group, 2 * QS), jnp.bfloat16),
                    pltpu.VMEM(
                        (PERIOD // LANES, RADIX * segments * group, 2 * LANES),
                        jnp.float32,
                    ),
                ),
            )
        )
    stack = jnp.stack(stacks)

    def from_window(array, flip):
        return lax.ppermute(array, "win", [(w, w ^ flip) for w in range(windows)])

    for step in (1 << i for i in range(2, windows.bit_length() - 1)):
        stack = call(
            add_kernel,
            jax.ShapeDtypeStruct(stack.shape, jnp.float32),
            stack,
            from_window(stack, step),
        )
    result = call(
        result_kernel,
        jax.ShapeDtypeStruct((offsets, group, PERIOD), jnp.float32),
        from_window(stack, 1),
        from_window(stack, 3),
        square,
    )
    return call(
        functools.partial(join_kernel, blocks),
        jax.ShapeDtypeStruct((1, 2 * offsets, channels, channels, LAGS), jnp.float32),
        result,
        to_mate(result),
    )


def solution(mesh):
    placed = (P(("arrays", "chan"), "win", None, None), P("arrays"))
    return jax.shard_map(
        shards,
        mesh=mesh,
        in_specs=placed,
        out_specs=P(("arrays", "chan"), None, None, None, None),
        check_vma=False,
    )
```

```python
import functools
import math

import jax
import jax.numpy as jnp
import numpy as np
from jax import lax
from jax.experimental import pallas as pl
from jax.experimental.pallas import tpu as pltpu
from jax.sharding import PartitionSpec as P

NFFT = 2048
F = 512
LAGS = 1024
LOWEST = NFFT // 16
LANES = 128

RADIX = 4
PERIOD = NFFT // RADIX
QS = F // RADIX
SPLIT = 8
SPAN = NFFT // SPLIT
NARROW = F // SPLIT
FORWARD_Q = LOWEST // SPLIT + np.arange(NARROW)
BACKWARD_Q = np.concatenate([2 * FORWARD_Q, 2 * FORWARD_Q + 1])

VMEM = pl.BlockSpec(memory_space=pltpu.VMEM)
HBM = pl.BlockSpec(memory_space=pltpu.HBM)


def side(block, core, blocks):
    return (core + block // (blocks // 2)) % 2


def split_three(table):
    parts = []
    rest = np.asarray(table, np.float64)
    for _ in range(3):
        part = rest.astype(np.float32).astype(jnp.bfloat16)
        parts.append(part)
        rest = rest - part.astype(np.float64)
    return parts


def forward_table():
    t0 = np.arange(SPAN)
    angle = (t0[:, None] * FORWARD_Q[None, :] % SPAN) * (2 * math.pi / SPAN)
    parts = split_three(np.block([np.cos(angle), np.sin(angle)]))
    return np.concatenate(parts, axis=1)


def backward_table():
    m = np.arange(PERIOD)
    angle = (BACKWARD_Q[:, None] * m[None, :] % PERIOD) * (2 * math.pi / PERIOD)
    cosine, sine = np.cos(angle), np.sin(angle)
    halves = np.array([np.block([[cosine], [-sine]]), np.block([[sine], [cosine]])])
    table = halves.reshape(2, 2 * QS, -1, LANES).transpose(1, 2, 0, 3)
    table = table.reshape(2 * QS, 2 * PERIOD) / math.sqrt(F)
    return table.astype(np.float32).astype(jnp.bfloat16)


def twiddles(count, length):
    n = np.arange(length)
    rows = []
    for r in range(1, count):
        angle = (r * n) * (2 * math.pi / NFFT)
        rows += [np.cos(angle), np.sin(angle)]
    rows += [np.zeros(length)] * 2
    return np.stack(rows).astype(np.float32)


def eight_points(x):
    half = math.sqrt(0.5)
    s04, d04, s26, d26 = x[0] + x[4], x[0] - x[4], x[2] + x[6], x[2] - x[6]
    s15, d15, s37, d37 = x[1] + x[5], x[1] - x[5], x[3] + x[7], x[3] - x[7]
    even, odd = s04 + s26, s15 + s37
    plus, minus = (d15 + d37) * half, (d15 - d37) * half
    two = s04 - s26, s37 - s15
    one = d04 + minus, -(d26 + plus)
    three = d04 - minus, d26 - plus
    return [
        (even + odd, None),
        one,
        two,
        three,
        (even - odd, None),
        (three[0], -three[1]),
        (two[0], -two[1]),
        (one[0], -one[1]),
    ]


def whiten_kernel(
    rows,
    pairs,
    x_hbm,
    table_hbm,
    twiddle_hbm,
    count_hbm,
    backward_hbm,
    backward_twiddle_hbm,
    out_ref,
    kept_ref,
    square_ref,
    backward_ref,
    backward_twiddle_ref,
    x_ref,
    table,
    twiddle_ref,
    count_ref,
    sems,
):
    copies = [
        pltpu.make_async_copy(twiddle_hbm, twiddle_ref, sems.at[1]),
        pltpu.make_async_copy(table_hbm, table, sems.at[2]),
        pltpu.make_async_copy(count_hbm, count_ref, sems.at[3]),
    ]
    piece = x_ref.shape[0] // 4
    for i in range(4):
        at = pl.ds(i * piece, piece)
        copies.append(
            pltpu.make_async_copy(x_hbm.at[at], x_ref.at[at], sems.at[6 + i])
        )
    later = [
        pltpu.make_async_copy(backward_hbm, backward_ref, sems.at[4]),
        pltpu.make_async_copy(backward_twiddle_hbm, backward_twiddle_ref, sems.at[5]),
    ]
    copies = copies[3:] + copies[:3]
    for copy in copies + later:
        copy.start()
    for copy in copies:
        copy.wait()

    window = lax.axis_index("win")
    mate = window + 1 - 2 * (window % 2)
    counts = count_ref[...]
    lane = lax.broadcasted_iota(jnp.int32, counts.shape, 1)
    own_count, mate_count = (
        jnp.sum(jnp.where(lane == w, counts, 0), axis=1, keepdims=True)
        for w in (window, mate)
    )
    group = 2 * pairs
    is_own = lax.broadcasted_iota(jnp.int32, (group, LANES), 0) < pairs
    count = jnp.where(is_own, own_count, mate_count)
    for k in range(kept_ref.shape[0] // group):
        kept_ref[k * group : (k + 1) * group] = (count > k).astype(jnp.float32)
    total = jnp.sum(counts, axis=1, keepdims=True).astype(jnp.float32)
    square_ref[...] = jnp.broadcast_to(total * total, square_ref.shape)

    chunks = SPAN // LANES
    real = [[] for _ in range(SPLIT)]
    imag = [[] for _ in range(SPLIT)]
    for c in range(chunks):
        x = [
            x_ref[pl.ds(t1 * chunks + c, rows, stride=SPLIT * chunks), :]
            for t1 in range(SPLIT)
        ]
        for r, (re, im) in enumerate(eight_points(x)):
            if r > 0:
                cosine, sine = (
                    twiddle_ref[2 * r - 2 + i : 2 * r - 1 + i, c * LANES : (c + 1) * LANES]
                    for i in range(2)
                )
                if im is None:
                    re, im = re * cosine, -(re * sine)
                else:
                    re, im = re * cosine + im * sine, im * cosine - re * sine
                imag[r].append(im)
            real[r].append(re)
    series = jnp.concatenate(
        [jnp.concatenate(part, axis=1) for part in real + imag[1:]], axis=0
    )
    high = series.astype(jnp.bfloat16)
    rest = series - high.astype(jnp.float32)
    mid = rest.astype(jnp.bfloat16)
    low = (rest - mid.astype(jnp.float32)).astype(jnp.bfloat16)
    dot = functools.partial(jnp.dot, preferred_element_type=jnp.float32)
    width = 2 * NARROW
    n = series.shape[0]
    both = dot(jnp.concatenate([high, mid, low], axis=0), table[:, : 2 * width])
    small = dot(high, table[:, 2 * width :])
    small = small + (both[n : 2 * n, width:] + both[2 * n :, :width])
    product = both[:n, :width] + ((both[:n, width:] + both[n : 2 * n, :width]) + small)
    left = lax.broadcasted_iota(jnp.int32, (rows, LANES), 1) < NARROW
    blocks = []
    for r in range(SPLIT):
        block = product[r * rows : (r + 1) * rows]
        block = jnp.where(left, block, -block)
        if r > 0:
            at = (SPLIT + r - 1) * rows
            block = block + pltpu.roll(product[at : at + rows], NARROW, axis=1)
        blocks.append(block)
    power = []
    for block in blocks:
        square = block * block
        power.append(square + pltpu.roll(square, NARROW, axis=1))
    total = ((power[0] + power[1]) + (power[2] + power[3])) + (
        (power[4] + power[5]) + (power[6] + power[7])
    )
    mean = jnp.sum(total, axis=1, keepdims=True) * (0.5 / F)
    most = lax.rsqrt(0.09 * (mean + 1e-06))
    white = [
        b * jnp.minimum(lax.rsqrt(jnp.maximum(p, 1e-08)), most)
        for b, p in zip(blocks, power)
    ]
    for r in range(RADIX):
        first, second = white[r], white[r + RADIX]
        at = 2 * r * QS
        re = jnp.where(left, first, pltpu.roll(second, NARROW, axis=1))
        im = jnp.where(left, pltpu.roll(first, NARROW, axis=1), second)
        out_ref[:, at : at + QS] = re.astype(jnp.bfloat16)
        out_ref[:, at + QS : at + 2 * QS] = im.astype(jnp.bfloat16)
    for copy in later:
        copy.wait()


def stack_kernel(
    channels,
    segments,
    own_ref,
    own_mate_ref,
    second_ref,
    first_ref,
    kept_ref,
    table_ref,
    twiddle_ref,
    out_ref,
    own,
    visitor,
    cross,
    inner,
):
    rows = channels * segments
    pairs = channels * channels
    group = 2 * pairs
    own[0:rows] = own_ref[...].astype(jnp.float32)
    own[rows : 2 * rows] = own_mate_ref[...].astype(jnp.float32)
    mine = (lax.axis_index("chan") + lax.axis_index("win")) % 2 == 0
    at = jnp.where(mine, 0, rows)
    for ref, start in ((first_ref, at), (second_ref, rows - at)):
        start = pl.multiple_of(start, 8)
        visitor[pl.ds(start, rows)] = ref[...].astype(jnp.float32)

    place = lax.broadcasted_iota(jnp.int32, (group, LANES), 0)
    own_of = place // channels
    visitor_of = place // pairs * channels + place % channels
    is_own = place < pairs

    def spread(ref, choice, segment, at):
        value = None
        for i in range(2 * channels):
            row = ref[pl.ds(i * segments + segment, 1), pl.ds(at, LANES)]
            row = jnp.broadcast_to(row, (group, LANES))
            value = row if value is None else jnp.where(choice == i, row, value)
        return value

    kept = [kept_ref[k * group : (k + 1) * group] for k in range(segments)]

    for r in range(RADIX):
        cross_real, cross_imag = [], []
        at = 2 * r * QS
        for k in range(segments):
            own_re = spread(own, own_of, k, at)
            own_im = spread(own, own_of, k, at + QS)
            vis_re = spread(visitor, visitor_of, k, at)
            vis_im = spread(visitor, visitor_of, k, at + QS)
            vis_re, vis_im = vis_re * kept[k], vis_im * kept[k]
            cross_real.append(own_re * vis_re + own_im * vis_im)
            cross_imag.append(own_im * vis_re - own_re * vis_im)
        at = slice(r * segments * group, (r + 1) * segments * group)
        cross[at, 0:QS] = jnp.concatenate(cross_real, axis=0).astype(jnp.bfloat16)
        cross[at, QS:] = jnp.concatenate(cross_imag, axis=0).astype(jnp.bfloat16)

    def product(c):
        inner[c] = jnp.dot(
            cross[...],
            table_ref[:, 2 * c * LANES : 2 * (c + 1) * LANES],
            preferred_element_type=jnp.float32,
        )

    product(0)
    for c in range(PERIOD // LANES):
        if c + 1 < PERIOD // LANES:
            product(c + 1)
        low, high = c * LANES, (c + 1) * LANES
        cos1, sin1, cos2, sin2, cos3, sin3 = (
            jnp.broadcast_to(twiddle_ref[i : i + 1, low:high], (group, LANES))
            for i in range(6)
        )
        sums = [[None] * 3, [None] * 3]
        for k in range(segments):
            re, im = (
                [
                    inner[c, pl.ds((r * segments + k) * group, group), half]
                    for r in range(RADIX)
                ]
                for half in (slice(0, LANES), slice(LANES, 2 * LANES))
            )
            re1, im1 = re[1] * cos1 - im[1] * sin1, re[1] * sin1 + im[1] * cos1
            re2, im2 = re[2] * cos2 - im[2] * sin2, re[2] * sin2 + im[2] * cos2
            re3, im3 = re[3] * cos3 - im[3] * sin3, re[3] * sin3 + im[3] * cos3
            later = (re[0] + re2) + (re1 + re3), (im[0] + im2) + (im1 + im3)
            earlier = (re[0] - re2) + (im1 - im3), (im[0] - im2) - (re1 - re3)
            for half, (direct, quadrature) in enumerate((earlier, later)):
                power = direct * direct + quadrature * quadrature
                scale = lax.rsqrt(jnp.maximum(power, 0.25))
                terms = (direct, direct * scale, quadrature * scale)
                for i, term in enumerate(terms):
                    old = sums[half][i]
                    sums[half][i] = term if old is None else old + term
        for i in range(3):
            first, second = (
                sums[half][i] + pltpu.roll(sums[half][i], pairs, axis=0)
                for half in range(2)
            )
            out_ref[i * group : (i + 1) * group, low:high] = jnp.where(
                is_own, first, second
            )


def add_kernel(left_ref, right_ref, out_ref):
    out_ref[...] = left_ref[...] + right_ref[...]


def result_kernel(left_ref, right_ref, square_ref, out_ref):
    group = out_ref.shape[1]
    for offset in range(out_ref.shape[0]):
        for low in range(0, out_ref.shape[2], LANES):
            at = slice(low, low + LANES)
            linear, cos_sum, sin_sum = (
                left_ref[offset, i * group : (i + 1) * group, at]
                + right_ref[offset, i * group : (i + 1) * group, at]
                for i in range(3)
            )
            power = cos_sum * cos_sum + sin_sum * sin_sum
            out_ref[offset, :, at] = linear * power / square_ref[...]


def join_kernel(blocks, own_ref, mate_ref, out_ref):
    parity = side(lax.axis_index("chan"), lax.axis_index("win") % 2, blocks)
    channels = out_ref.shape[2]
    half_lags = own_ref.shape[2]
    for ref, place in ((own_ref, 1 - parity), (mate_ref, parity)):
        for offset in range(own_ref.shape[0]):
            for half in range(2):
                for a in range(channels):
                    row = (half * channels + a) * channels
                    lags = slice(half * half_lags, (half + 1) * half_lags)
                    out_ref[0, 2 * offset + place, a, :, lags] = ref[
                        offset, row : row + channels
                    ]


def call(kernel, out, *args, specs=None, scratch=(), limit=8 << 20):
    return pl.pallas_call(
        kernel,
        out_shape=out,
        in_specs=[VMEM] * len(args) if specs is None else specs,
        out_specs=jax.tree.map(lambda _: VMEM, out),
        scratch_shapes=list(scratch),
        compiler_params=pltpu.CompilerParams(vmem_limit_bytes=limit),
    )(*args)


def shards(traces, seg_count):
    channels, _, segments, _ = traces.shape
    rows = channels * segments
    blocks = lax.axis_size("chan")
    windows = lax.axis_size("win")
    offsets = blocks // 4
    pairs = channels * channels
    group = 2 * pairs
    forward_twiddle = jnp.asarray(twiddles(SPLIT, SPAN))
    twiddle = jnp.asarray(twiddles(RADIX, PERIOD))
    forward = jnp.asarray(forward_table())
    series = traces.reshape(-1, LANES)

    counts = seg_count.reshape(1, -1)
    backward = jnp.asarray(backward_table())
    inputs = (series, forward, forward_twiddle, counts)
    inputs_on = (backward, twiddle)
    own, kept, square, backward, twiddle = call(
        functools.partial(whiten_kernel, rows, pairs),
        (
            jax.ShapeDtypeStruct((rows, 2 * F), jnp.bfloat16),
            jax.ShapeDtypeStruct((segments * group, LANES), jnp.float32),
            jax.ShapeDtypeStruct((group, LANES), jnp.float32),
            *(jax.ShapeDtypeStruct(x.shape, x.dtype) for x in inputs_on),
        ),
        *(pltpu.with_memory_space_constraint(x, pltpu.HBM) for x in inputs + inputs_on),
        specs=[HBM] * 6,
        scratch=(
            *(pltpu.VMEM(x.shape, x.dtype) for x in inputs),
            pltpu.SemaphoreType.DMA((10,)),
        ),
    )

    def to_mate(array):
        return lax.ppermute(array, "win", [(w, w ^ 1) for w in range(windows)])

    def from_block(array, offset, flip):
        moves = []
        for z in range(blocks):
            for w in range(windows):
                block = (z + offset + side(z, w % 2, blocks)) % blocks
                source = block * windows + w // 2 * 2 + (z % 2 ^ flip)
                moves.append((source, z * windows + w))
        return lax.ppermute(array, ("chan", "win"), moves)

    own_mate = to_mate(own)
    stacks = []
    for j in range(offsets):
        second = from_block(own, 1 + 2 * j, 1)
        first = from_block(own, 1 + 2 * j, 0)
        stacks.append(
            call(
                functools.partial(stack_kernel, channels, segments),
                jax.ShapeDtypeStruct((3 * group, PERIOD), jnp.float32),
                own,
                own_mate,
                second,
                first,
                kept,
                backward,
                twiddle,
                scratch=(
                    pltpu.VMEM((2 * rows, 2 * F), jnp.float32),
                    pltpu.VMEM((2 * rows, 2 * F), jnp.float32),
                    pltpu.VMEM((RADIX * segments * group, 2 * QS), jnp.bfloat16),
                    pltpu.VMEM(
                        (PERIOD // LANES, RADIX * segments * group, 2 * LANES),
                        jnp.float32,
                    ),
                ),
            )
        )
    stack = jnp.stack(stacks)

    def from_window(array, flip):
        return lax.ppermute(array, "win", [(w, w ^ flip) for w in range(windows)])

    for step in (1 << i for i in range(2, windows.bit_length() - 1)):
        stack = call(
            add_kernel,
            jax.ShapeDtypeStruct(stack.shape, jnp.float32),
            stack,
            from_window(stack, step),
        )
    result = call(
        result_kernel,
        jax.ShapeDtypeStruct((offsets, group, PERIOD), jnp.float32),
        from_window(stack, 1),
        from_window(stack, 3),
        square,
    )
    return call(
        functools.partial(join_kernel, blocks),
        jax.ShapeDtypeStruct((1, 2 * offsets, channels, channels, LAGS), jnp.float32),
        result,
        to_mate(result),
    )


def solution(mesh):
    placed = (P(("arrays", "chan"), "win", None, None), P("arrays"))
    return jax.shard_map(
        shards,
        mesh=mesh,
        in_specs=placed,
        out_specs=P(("arrays", "chan"), None, None, None, None),
        check_vma=False,
    )
```
